32 devices in a mesh: rep: 2 (over x), seq: 16 (over z, y, core).
Axes of the slice: x: 2, y: 2, z: 4, core: 2. Of those that a mesh axis runs over, the one named last changes fastest.
Arguments:
- cached_keys: bfloat16 [32768, 1024], P(('rep', 'seq')), parts along dimension 0, may hold values from -6 to 6
- cached_values: bfloat16 [32768, 1024], P(('rep', 'seq')), parts along dimension 0, may hold values from -6 to 6
- window_queries: bfloat16 [256, 8192], P(('rep', 'seq')), parts along dimension 0
- kept_count: int32 [32], P(('rep', 'seq')), parts along dimension 0, may hold values from 1 to 640, 8192 in all
- kept_entry: int32 [20480], P(('rep', 'seq')), parts along dimension 0, may hold values from 0 to 8191
- row_owner: int32 [20480], P(('rep', 'seq')), parts along dimension 0, may hold values from 0 to 15, as said below
Outputs:
- importance: float32 [16, 16384], P('rep', 'seq'), parts along dimension 0
- compact_rows: bfloat16 [20480, 256], P(('rep', 'seq')), parts along dimension 0
- compact_score: bfloat16 [20480], P(('rep', 'seq')), parts along dimension 0
The draws below stay inside these ranges and needn't reach their ends.
There are 2 independent parts, one for each index of `rep`. The reference program is written for one: setup_inputs(seed, part) draws one part's arguments, and reference() takes and returns one part's arrays. A program takes and returns all parts, laid end to end along the dimension named above; each array names one. Nothing has to cross between parts.
Inputs may be any that keep to these rules, and one draw needn't show every extreme that they name: `kept_count`: the counts of the 16 devices sum to 8192. `kept_entry`: entries may repeat. `row_owner`: among the 640 slots of one device every owner is named by exactly 40 slots.
All inputs are finite; a program needn't handle non-finite values.
Results may differ from the reference program's by a relative error of at most 0.0004.
Values may be sent and summed in bfloat16 or wider, within the bound.
A program may use at most 64 MiB of HBM per device.

```python
import math
import jax
import jax.numpy as jnp
import numpy as np
from jax import lax

HEADS = 64
KV_HEADS = 8
HEAD_DIM = 128
GROUP = 8
WINDOW = 128
POOL = 7
TOK_DEV = 1024
SEQ = 16384
SLOTS = 640
CAP = 40
KEPT = 8192
N_SEQ = 16


def draw_cached_keys(key, part):
    return jnp.clip(jax.random.normal(jax.random.fold_in(key, 3), (SEQ, KV_HEADS * HEAD_DIM), jnp.float32), -6.0, 6.0).astype(jnp.bfloat16)


def draw_window_queries(key, part):
    return jnp.clip(jax.random.normal(jax.random.fold_in(key, 5), (WINDOW, HEADS * HEAD_DIM), jnp.float32), -6.0, 6.0).astype(jnp.bfloat16)


def draw_row_owner(key, part):
    peers = N_SEQ
    filled = jnp.tile(jnp.arange(peers, dtype=jnp.int32)[None, :], (peers, CAP))
    shuffle = jax.random.randint(jax.random.fold_in(key, 23), (peers, SLOTS), 0, 2 ** 19) * SLOTS + jnp.arange(SLOTS)[None, :]
    order = jnp.argsort(shuffle, axis=1, stable=True)
    return jnp.take_along_axis(filled, order, axis=1).reshape(-1).astype(jnp.int32)


def set_ends(values, own_key, smallest, top_value):
    longest = values.shape.index(max(values.shape))
    spots = []
    for shift in (0, 1):
        where = [jax.random.randint(jax.random.fold_in(own_key, axis), (), 0, length) for axis, length in enumerate(values.shape)]
        where[longest] = (where[longest] + shift) % values.shape[longest]
        spots.append(tuple(where))
    return values.at[spots[0]].set(smallest).at[spots[1]].set(top_value)


def levels(key, shape, pieces, low, largest):
    gain, own = 1.0, jax.random.fold_in(key, 6)
    for position, blocks in pieces:
        steps = jnp.exp(jax.random.uniform(jax.random.fold_in(own, position), (blocks,), jnp.float32, low / len(pieces), largest / len(pieces)))
        gain = gain * jnp.repeat(steps, shape[position] // blocks).reshape([-1 if axis == position else 1 for axis in range(len(shape))])
    return gain


def split_up(amount, total, bound, slope):
    portions = [(1 << 20) // math.isqrt(standing ** slope) + 1 for standing in range(2, amount + 1)]
    spare, given = total - bound - (amount - 1), [1] * (amount - 1)
    while spare > 0:
        candidates = [i for i in range(amount - 1) if given[i] < bound]
        pool, remaining = sum([portions[i] for i in candidates]), spare
        for i in candidates:
            addition = min(bound - given[i], max(1, remaining * portions[i] // pool), spare)
            given[i] = given[i] + addition
            spare = spare - addition
    return np.array([bound] + given)


def ragged_sizes(rng, number_of, total, most, slope):
    if number_of == 2:
        one = jax.random.randint(rng, (), max(1, total - most), min(most, total - 1) + 1)
        return jnp.stack([one, total - one])
    sizes = jnp.asarray(split_up(number_of, total, most, slope), jnp.int32)
    twos = (number_of - 1) // 2
    giver, sink = sizes[1:1 + 2 * twos:2], sizes[2:2 + 2 * twos:2]
    room = jnp.minimum(giver - 1, most - sink)
    moved = jax.random.randint(jax.random.fold_in(rng, 1), (twos,), 0, 1 << 20) % (room + 1)
    sizes = sizes.at[1:1 + 2 * twos:2].set(giver - moved).at[2:2 + 2 * twos:2].set(sink + moved)
    return sizes[jax.random.permutation(jax.random.fold_in(rng, 2), number_of)]


def bell_draw(rng, dims, spread, most, shards=(), kind=jnp.bfloat16):
    loudness = levels(rng, dims, shards, -0.22, 0.18) if shards else 1.0
    result = jax.random.normal(rng, dims, jnp.float32) * spread * loudness
    return jnp.minimum(jnp.maximum(result, -most), most).astype(kind)


def setup_inputs(seed: int = 0, part: int = 0) -> dict:
    splits = jax.random.split(jax.random.key(seed), 7)
    part_splits = jax.random.split(jax.random.fold_in(splits[6], part), 7)
    return {
        "cached_keys": draw_cached_keys(jax.random.fold_in(jax.random.fold_in(splits[6], part), 71), part),
        "cached_values": bell_draw(part_splits[1], (SEQ, KV_HEADS * HEAD_DIM), 1.0, 6.0, ((0, 16),)),
        "window_queries": draw_window_queries(jax.random.fold_in(jax.random.fold_in(splits[6], part), 71), part),
        "kept_count": ragged_sizes(part_splits[3], N_SEQ, KEPT, SLOTS, 2).astype(jnp.int32),
        "kept_entry": set_ends(jax.random.randint(part_splits[4], (N_SEQ * SLOTS,), 0, KV_HEADS * TOK_DEV), jax.random.fold_in(part_splits[4], 1), 0, (KV_HEADS * TOK_DEV) - 1).astype(jnp.int32),
        "row_owner": draw_row_owner(jax.random.fold_in(jax.random.fold_in(splits[6], part), 71), part),
    }


def window_groups(window_queries):
    shaped = window_queries.reshape(WINDOW, KV_HEADS, GROUP, HEAD_DIM).transpose(1, 2, 0, 3)
    return shaped.reshape(KV_HEADS, GROUP * WINDOW, HEAD_DIM).astype(jnp.float32)


def block_scores(query_groups, key_block):
    return jnp.einsum("gqd,gtd->gqt", query_groups, key_block.astype(jnp.float32)) * (HEAD_DIM ** -0.5)


def reference(cached_keys, cached_values, window_queries, kept_count, kept_entry, row_owner):
    query_groups = window_groups(window_queries)
    key_blocks = cached_keys.reshape(N_SEQ, TOK_DEV, KV_HEADS, HEAD_DIM).transpose(0, 2, 1, 3)

    def stat_step(carry, key_block):
        run_peak, run_total = carry
        scores = block_scores(query_groups, key_block)
        new_peak = jnp.maximum(run_peak, jnp.max(scores, axis=2))
        run_total = run_total * jnp.exp(run_peak - new_peak) + jnp.sum(jnp.exp(scores - new_peak[:, :, None]), axis=2)
        return (new_peak, run_total), None

    initial = (jnp.full((KV_HEADS, GROUP * WINDOW), -jnp.inf, jnp.float32), jnp.zeros((KV_HEADS, GROUP * WINDOW), jnp.float32))
    (glob_peak, glob_total), _ = lax.scan(stat_step, initial, key_blocks)
    inverse = 1.0 / glob_total

    def mass_step(carry, key_block):
        scores = block_scores(query_groups, key_block)
        return carry, jnp.sum(jnp.exp(scores - glob_peak[:, :, None]) * inverse[:, :, None], axis=1)

    _, column_mass = lax.scan(mass_step, jnp.zeros((), jnp.float32), key_blocks)
    column_mass = column_mass.transpose(1, 0, 2).reshape(KV_HEADS, SEQ)
    margin = POOL // 2
    padded = jnp.pad(column_mass, ((0, 0), (margin, margin)))
    pooled = padded[:, 0:SEQ]
    for offset in range(1, POOL):
        pooled = pooled + padded[:, offset:offset + SEQ]
    importance = pooled * (SEQ / (GROUP * WINDOW * POOL))

    everything = jnp.arange(N_SEQ * SLOTS, dtype=jnp.int32)
    device = everything // SLOTS
    within = everything % SLOTS
    is_live = within < kept_count[device]
    member = ((row_owner[:, None] == jnp.arange(N_SEQ, dtype=jnp.int32)[None, :]) & is_live[:, None]).astype(jnp.int32)
    member = member.reshape(N_SEQ, SLOTS, N_SEQ)
    earlier = jnp.cumsum(member, axis=1) - member
    slot_rank = jnp.sum(earlier * member, axis=2).reshape(-1)
    head_index = kept_entry // TOK_DEV
    token_index = device * TOK_DEV + kept_entry % TOK_DEV
    row_index = token_index * KV_HEADS + head_index
    key_rows = cached_keys.reshape(SEQ * KV_HEADS, HEAD_DIM)[row_index]
    value_rows = cached_values.reshape(SEQ * KV_HEADS, HEAD_DIM)[row_index]
    payload = jnp.concatenate([key_rows, value_rows], axis=1)
    score_rows = importance[head_index, token_index].astype(jnp.bfloat16)
    total_rows = N_SEQ * N_SEQ * CAP
    target = jnp.where(is_live, row_owner * (N_SEQ * CAP) + device * CAP + slot_rank, total_rows)
    compact_rows = jnp.zeros((total_rows, 2 * HEAD_DIM), jnp.bfloat16).at[target].set(payload, mode="drop")
    compact_score = jnp.zeros((total_rows,), jnp.bfloat16).at[target].set(score_rows, mode="drop")
    return importance, compact_rows, compact_score
```

```python
import functools

import jax
import jax.numpy as jnp
from jax import lax
from jax.experimental import pallas as pl
from jax.experimental.pallas import tpu as pltpu
from jax.sharding import PartitionSpec as P

KV_HEADS = 8
GROUP = 8
HEAD_DIM = 128
POOL = 7
LOG2E = 1.4426950408889634
LANES = 128
EDGE = 16
STRIP = 64
MESH = pl.DeviceIdType.MESH
NT = (((1,), (1,)), ((), ()))


def iota(shape, dim):
    return lax.broadcasted_iota(jnp.int32, shape, dim)


def kernel(
    n, cap, cap_pad, pool_scale,
    keys_hbm, vals_hbm, wq_hbm, count_hbm, entry_hbm, owner_hbm,
    imp_ref, rows_out, score_out,
    keys, vals, qall, ebuf, raw, peak, sums, stat, stat_in, stat_all, glob, rows_send, onehot, slot_tile, slot_lane,
    mass, edge, ssend, srecv, count_ref, entry_ref, owner_ref,
    zs, zr, ws, wr, ys, yr, bs, br, ts, tr, gs, gr, rs, rr, hs, hr, ss, sr, ls, es, er,
):
    G = KV_HEADS
    me = lax.axis_index("seq")
    A = n // 4
    A1 = A // 2
    a, b, c = me // 4, (me // 2) % 2, me % 2
    a1, a0 = a // 2, a % 2
    slots = entry_ref.shape[0]
    positions = vals.shape[0]
    tiles = positions // LANES
    out_slots = n * cap_pad
    queries = ebuf.shape[2]
    scale2 = HEAD_DIM ** (-0.5) * LOG2E
    per_owner = n // G

    def stat_owner(g):
        return (g * per_owner + n // 2) % n

    def to(index):
        return {"seq": index}

    def remote(src, dst, ssem, rsem, index):
        return pltpu.make_async_remote_copy(
            src_ref=src, dst_ref=dst, send_sem=ssem, recv_sem=rsem,
            device_id=to(index), device_id_type=MESH,
        )

    def drain(region, sem):
        pltpu.make_async_copy(region, region, sem).wait()

    barrier = pltpu.get_barrier_semaphore()

    @pl.loop(1, n)
    def _(k):
        pl.semaphore_signal(barrier, inc=1, device_id=to(lax.rem(me + k, n)), device_id_type=MESH)

    own_q = pltpu.make_async_copy(wq_hbm, qall.at[:, c, b, a0, a1], ls.at[2])
    small = [
        pltpu.make_async_copy(src, dst, ls.at[4 + i])
        for i, (src, dst) in enumerate(((count_hbm, count_ref), (entry_hbm, entry_ref), (owner_hbm, owner_ref)))
    ]
    key_copy = pltpu.make_async_copy(keys_hbm, keys.at[pl.ds(0, positions)], ls.at[0])
    val_copy = pltpu.make_async_copy(vals_hbm, vals, ls.at[1])
    own_q.start()
    for copy in small:
        copy.start()
    key_copy.start()
    val_copy.start()

    low, high = lax.rem(me + n - 1, n), lax.rem(me + 1, n)
    mid_peer = a * 4 + (1 - b) * 2 + c
    core_peer = a * 4 + b * 2 + (1 - c)
    step_peer = (a + 1 - 2 * a0) * 4 + b * 2 + c
    first_rows = pl.ds(0, EDGE)
    last_rows = pl.ds(positions - EDGE, EDGE)
    from_low = pl.ds(positions, EDGE)
    from_high = pl.ds(positions + EDGE, EDGE)

    @pl.when(me == 0)
    def _():
        keys[positions:positions + EDGE, :] = jnp.zeros((EDGE, keys.shape[1]), keys.dtype)

    @pl.when(me == n - 1)
    def _():
        keys[positions + EDGE:positions + 2 * EDGE, :] = jnp.zeros((EDGE, keys.shape[1]), keys.dtype)

    def greet():
        own_q.wait()
        pl.semaphore_wait(barrier, n - 1)

        @pl.loop(0, G)
        def _(g):
            mine = qall.at[g, c, b, a0, a1]

            @pl.loop(1, A1)
            def _(k):
                peer = (lax.rem(a1 + k, A1) * 2 + a0) * 4 + b * 2 + c
                remote(mine, mine, zs.at[g], zr.at[g], peer).start()

            remote(mine, mine, ys.at[g], yr.at[g], mid_peer).start()

        @pl.when(me > 0)
        def _():
            remote(keys_hbm.at[first_rows], keys.at[from_high], hs.at[0], hr.at[0], low).start()

        @pl.when(me < n - 1)
        def _():
            remote(keys_hbm.at[last_rows], keys.at[from_low], hs.at[1], hr.at[1], high).start()

    late = me >= n // 2

    @pl.when(late)
    def _():
        greet()

    for copy in small:
        copy.wait()
    entry = entry_ref[...].reshape(1, slots)
    owner = owner_ref[...].reshape(1, slots)
    live = iota((1, slots), 1) < count_ref[0]
    owner_live = jnp.where(live, owner, -1)
    member = jnp.where(iota((n, slots), 0) == owner_live, 1.0, 0.0)
    before = jnp.where(iota((slots, slots), 0) < iota((slots, slots), 1), 1.0, 0.0).astype(jnp.bfloat16)
    earlier = jnp.dot(member.astype(jnp.bfloat16), before, preferred_element_type=jnp.float32)
    rank = jnp.sum(member * earlier, axis=0, keepdims=True).astype(jnp.int32)
    target = jnp.where(live, owner * cap_pad + rank, -1)
    tile_of = entry // LANES
    lane_of = entry - tile_of * LANES
    head = tile_of // tiles
    token_f = (entry - head * positions + 1).astype(jnp.float32)
    head_f = head.astype(jnp.float32)
    at_rank = jnp.where(iota((LANES, slots), 0) == rank, 1.0, 0.0).astype(jnp.bfloat16)

    def by_rank(value):
        marked = (member * value.astype(jnp.float32)).astype(jnp.bfloat16)
        return lax.dot_general(marked, at_rank, NT, preferred_element_type=jnp.float32).astype(jnp.int32)

    slot_tile[...] = by_rank(tile_of + 1)
    slot_lane[...] = by_rank(lane_of)

    @pl.when(jnp.logical_not(late))
    def _():
        greet()

    key_copy.wait()
    val_copy.wait()

    def gather_rows(k0, count):
        blk = count * cap_pad
        hit = (iota((blk, slots), 0) + k0 * cap_pad) == target
        tok = jnp.sum(jnp.where(hit, token_f, 0.0), axis=1, keepdims=True).astype(jnp.int32) - 1
        hcol = jnp.sum(jnp.where(hit, head_f, 0.0), axis=1, keepdims=True).astype(jnp.int32)
        hcol = jnp.broadcast_to(hcol, (blk, HEAD_DIM))
        onehot[...] = jnp.where(iota((blk, positions), 1) == tok, 1.0, 0.0).astype(jnp.bfloat16)
        for side, source in enumerate((keys, vals)):
            got = jnp.dot(onehot[...], source[0:positions, :], preferred_element_type=jnp.float32)
            chosen = jnp.zeros((blk, HEAD_DIM), jnp.float32)
            for h in range(G):
                chosen = jnp.where(hcol == h, got[:, h * HEAD_DIM:(h + 1) * HEAD_DIM], chosen)
            for k in range(count):
                rows_send[k0 + k, :, side * HEAD_DIM:(side + 1) * HEAD_DIM] = chosen[
                    k * cap_pad:(k + 1) * cap_pad
                ].astype(jnp.bfloat16)

    per = onehot.shape[0] // cap_pad
    for i in range(n // per):
        gather_rows(i * per, per)

    def lse(values):
        top = values[0]
        for x in values[1:]:
            top = jnp.maximum(top, x)
        total = jnp.zeros_like(top)
        for x in values:
            total = total + jnp.exp2(x - top)
        return top + jnp.log(total) * LOG2E

    def join(g, gathered):
        gathered[me] = stat[g]
        glob[g] = lse([gathered[d] for d in range(n)])

    def combine(g):
        @pl.when(me == stat_owner(g))
        def _():
            drain(stat_in.at[pl.ds(0, n - 1)], tr.at[0])
            join(g, stat_in)

            @pl.loop(1, n)
            def _(k):
                remote(glob.at[g], glob.at[g], gs.at[0], gr.at[g], lax.rem(me + k, n)).start()

    chunk = 2 * LANES
    strip = sums.shape[0]
    span = positions // strip

    def compute(g):
        group_q = qall.at[g].reshape(queries, HEAD_DIM)
        key_cols = pl.ds(pl.multiple_of(g * HEAD_DIM, HEAD_DIM), HEAD_DIM)
        for j in range(queries // chunk):
            lanes = slice(j * chunk, (j + 1) * chunk)
            s = lax.dot_general(
                keys[:, key_cols], group_q[lanes, :], NT, preferred_element_type=jnp.float32
            )
            for u in range(strip):
                x = s[u * span:(u + 1) * span].reshape(span // 8, 8, chunk)
                top = jnp.max(x, axis=0)
                e = jnp.exp2((x - top[None]) * scale2)
                ebuf[g, u * span:(u + 1) * span, lanes] = e.reshape(span, chunk)
                peak[g, u, :, lanes] = top
                sums[u, :, lanes] = jnp.sum(e, axis=0)
            raw[g, 0:8, lanes] = s[positions + EDGE - 8:positions + EDGE]
            raw[g, 8:16, lanes] = s[positions + EDGE:positions + EDGE + 8]
        tops = peak[g]
        top = jnp.max(jnp.max(tops, axis=0), axis=0, keepdims=True)
        total = jnp.sum(jnp.sum(sums[...] * jnp.exp2((tops - top[None]) * scale2), axis=0), axis=0, keepdims=True)
        local = top * scale2 + jnp.log(total) * LOG2E
        for i in range(queries // LANES):
            stat[g, i:i + 1, :] = local[:, i * LANES:(i + 1) * LANES]

        dest = stat_owner(g)

        @pl.when((g < G - 1) & (me != dest))
        def _():
            remote(stat.at[g], stat_in.at[me], ts.at[g], tr.at[0], dest).start()

        @pl.when(g == G - 1)
        def _():
            @pl.loop(1, n)
            def _(k):
                remote(stat.at[g], stat_all.at[me], es.at[0], er.at[0], lax.rem(me + k, n)).start()

    own_rows = pltpu.make_async_copy(rows_send.at[me], rows_out.at[me], ls.at[3])
    own_rows.start()

    lag = 8

    @pl.loop(0, G + 5)
    def _(step):
        @pl.when(step < G)
        def _():
            g = step
            drain(qall.at[g, c, b, a0, pl.ds(0, A1 - 1)], zr.at[g])
            mine = qall.at[g, c, b, a0]
            remote(mine, mine, ws.at[g], wr.at[g], step_peer).start()

            @pl.loop(1, A1)
            def _(k):
                other = qall.at[g, c, b, a0, lax.rem(a1 + k, A1)]
                remote(other, other, ys.at[g], yr.at[g], mid_peer).start()

        @pl.when((step >= 2) & (step < G + 2))
        def _():
            g = step - 2
            drain(qall.at[g, c, b, 1 - a0], wr.at[g])
            other = qall.at[g, c, b, 1 - a0]
            remote(other, other, ys.at[g], yr.at[g], mid_peer).start()

        @pl.when((step >= 4) & (step < G + 4))
        def _():
            g = step - 4
            drain(qall.at[g, c, 1 - b], yr.at[g])
            remote(qall.at[g, c], qall.at[g, c], bs.at[g], br.at[g], core_peer).start()

        @pl.when(step == G + 1)
        def _():
            @pl.loop(1, n)
            def _(k):
                peer = lax.rem(me + k, n)
                remote(rows_send.at[peer], rows_out.at[me], rs.at[0], rr.at[0], peer).start()

        @pl.when((step == 5) & (me < n - 1))
        def _():
            drain(keys.at[from_high], hr.at[0])

        @pl.when((step == 5) & (me > 0))
        def _():
            drain(keys.at[from_low], hr.at[1])

        @pl.when(step >= 5)
        def _():
            g = step - 5
            drain(qall.at[g, 1 - c], br.at[g])
            compute(g)

        @pl.when(step >= lag)
        def _():
            combine(step - lag)

    @pl.loop(G + 5 - lag, G - 1)
    def _(g):
        combine(g)

    @pl.loop(0, G)
    def _(g):
        @pl.when((g < G - 1) & (me != stat_owner(g)))
        def _():
            drain(glob.at[g], gr.at[g])

        @pl.when(g == G - 1)
        def _():
            drain(stat_all.at[pl.ds(0, n - 1)], er.at[0])
            join(g, stat_all)

        whole = glob[g]
        level = [whole[k:k + 1, :] for k in range(queries // LANES)]

        def weighted(value, k):
            return value * weight[:, k * LANES:(k + 1) * LANES][None]

        for t in range(tiles):
            acc = None
            for u in range(t * LANES // span, max((t + 1) * LANES // span, t * LANES // span + 1)):
                weight = jnp.concatenate(
                    [
                        jnp.exp2(peak[g, u, :, k * LANES:(k + 1) * LANES] * scale2 - level[k])
                        for k in range(queries // LANES)
                    ],
                    axis=1,
                )
                r0 = max(u * span, t * LANES)
                rows = min(span, LANES)
                part = None
                for k in range(queries // LANES):
                    e = ebuf[g, r0:r0 + rows, k * LANES:(k + 1) * LANES].reshape(rows // 8, 8, LANES)
                    e = weighted(e, k)
                    part = e if part is None else part + e
                part = part.reshape(rows, LANES)
                acc = part if acc is None else jnp.concatenate([acc, part], axis=0)
            mass[g, :, t * LANES:(t + 1) * LANES] = jnp.sum(acc.T, axis=0, keepdims=True)
        acc = None
        for k in range(queries // LANES):
            e = jnp.exp2(raw[g, :, k * LANES:(k + 1) * LANES] * scale2 - level[k])
            acc = e if acc is None else acc + e
        edge[pl.ds(pl.multiple_of(g * 16, 16), 16), :] = acc

    column = jnp.concatenate([mass[g] for g in range(G)], axis=0)
    line = jnp.sum(edge[...].T, axis=0, keepdims=True)
    row_of = iota((G, LANES), 0)
    ends = jnp.zeros((G, LANES), jnp.float32)
    for g in range(G):
        turned = pltpu.roll(line, (LANES - 8 - 16 * g) % LANES, 1)
        ends = jnp.where(row_of == g, turned, ends)
    before_low = jnp.where(me > 0, ends, 0.0)
    after_high = jnp.where(me < n - 1, ends, 0.0)
    padded = jnp.concatenate([before_low, column, after_high], axis=1)
    width = padded.shape[1]
    pooled = padded
    for o in range(1, POOL // 2 + 1):
        pooled = pooled + pltpu.roll(padded, o, 1) + pltpu.roll(padded, width - o, 1)
    importance = pooled[:, LANES:LANES + positions] * pool_scale
    imp_ref[...] = importance

    want, lane = slot_tile[...], slot_lane[...]
    table = jnp.zeros((n, LANES), jnp.float32)
    for h in range(G):
        for t in range(tiles):
            part = jnp.broadcast_to(importance[h:h + 1, t * LANES:(t + 1) * LANES], (n, LANES))
            found = jnp.take_along_axis(part, lane, axis=1)
            table = jnp.where(want == h * tiles + t + 1, found, table)
    for k in range(n):
        ssend[k] = table[k:k + 1, :]

    @pl.loop(1, n)
    def _(k):
        peer = lax.rem(me + k, n)
        remote(ssend.at[peer], srecv.at[me], ss.at[0], sr.at[0], peer).start()

    own_rows.wait()
    drain(rows_out.at[pl.ds(0, n - 1)], rr.at[0])
    drain(rows_send.at[pl.ds(0, n - 1)], rs.at[0])

    @pl.loop(0, G)
    def _(g):
        drain(qall.at[g, c, b, a0, pl.ds(0, A1 - 1)], zs.at[g])
        drain(qall.at[g, c, b, a0], ws.at[g])
        drain(qall.at[g, c, b], ys.at[g])
        drain(qall.at[g, c], bs.at[g])

        @pl.when((g < G - 1) & (me != stat_owner(g)))
        def _():
            drain(stat.at[g], ts.at[g])

        @pl.when((g < G - 1) & (me == stat_owner(g)))
        def _():
            drain(stat_in.at[pl.ds(0, n - 1)], gs.at[0])

    @pl.when(me > 0)
    def _():
        drain(keys.at[from_high], hs.at[0])

    @pl.when(me < n - 1)
    def _():
        drain(keys.at[from_low], hs.at[1])

    drain(stat_all.at[pl.ds(0, n - 1)], es.at[0])
    drain(ssend.at[pl.ds(0, n - 1)], ss.at[0])
    drain(srecv.at[pl.ds(0, n - 1)], sr.at[0])
    srecv[me] = ssend[me]
    score_out[...] = srecv[...]


def finish(cap, imp_in, rows_in, score_in, imp_ref, rows_ref, score_ref):
    n = rows_in.shape[0]
    imp_ref[...] = imp_in[...]
    rows_ref[...] = rows_in[:, 0:cap, :]
    table = jnp.concatenate([score_in[k] for k in range(n)], axis=0).astype(jnp.bfloat16)
    column = iota((LANES, n * cap), 1) - iota((LANES, n * cap), 0)
    unfold = jnp.where(column % cap == 0, 1.0, 0.0)
    unfold = jnp.where(iota((LANES, n * cap), 0) < cap, unfold, 0.0).astype(jnp.bfloat16)
    wide = jnp.dot(table, unfold, preferred_element_type=jnp.float32)
    within = iota((n, n * cap), 1) - iota((n, n * cap), 0) * cap
    line = jnp.sum(jnp.where((within >= 0) & (within < cap), wide, 0.0), axis=0, keepdims=True)
    score_ref[...] = line.astype(jnp.bfloat16).reshape(n * cap)


def per_device(n, cached_keys, cached_values, window_queries, kept_count, kept_entry, row_owner):
    positions, width = cached_keys.shape
    slots = kept_entry.shape[0]
    cap = slots // n
    cap_pad = -(-cap // 8) * 8
    query_rows = window_queries.shape[0]
    heads = window_queries.shape[1] // HEAD_DIM
    group = heads // KV_HEADS
    window = query_rows * n
    qrows = query_rows * group
    lane_rows = n * qrows // LANES
    wq = (
        window_queries.reshape(query_rows, heads, HEAD_DIM)
        .transpose(1, 0, 2)
        .reshape(KV_HEADS, qrows, HEAD_DIM)
    )
    pool_scale = n * positions / (group * window * POOL)
    any_spec = pl.BlockSpec(memory_space=pl.ANY)
    vmem = pl.BlockSpec(memory_space=pltpu.VMEM)
    dma = pltpu.SemaphoreType.DMA
    A = n // 4
    f32, bf16 = jnp.float32, jnp.bfloat16
    importance, rows, score = pl.pallas_call(
        functools.partial(kernel, n, cap, cap_pad, pool_scale),
        out_shape=(
            jax.ShapeDtypeStruct((KV_HEADS, positions), f32),
            jax.ShapeDtypeStruct((n, cap_pad, 2 * HEAD_DIM), bf16),
            jax.ShapeDtypeStruct((n, 1, LANES), f32),
        ),
        in_specs=[any_spec] * 6,
        out_specs=(vmem, any_spec, vmem),
        scratch_shapes=[
            pltpu.VMEM((positions + 2 * EDGE, width), bf16),
            pltpu.VMEM((positions, width), bf16),
            pltpu.VMEM((KV_HEADS, 2, 2, 2, A // 2, qrows, HEAD_DIM), bf16),
            pltpu.VMEM((KV_HEADS, positions, n * qrows), f32),
            pltpu.VMEM((KV_HEADS, 16, n * qrows), f32),
            pltpu.VMEM((KV_HEADS, positions // STRIP, 8, n * qrows), f32),
            pltpu.VMEM((positions // STRIP, 8, n * qrows), f32),
            pltpu.VMEM((KV_HEADS, lane_rows, LANES), f32),
            pltpu.VMEM((n, lane_rows, LANES), f32),
            pltpu.VMEM((n, lane_rows, LANES), f32),
            pltpu.VMEM((KV_HEADS, lane_rows, LANES), f32),
            pltpu.VMEM((n, cap_pad, 2 * HEAD_DIM), bf16),
            pltpu.VMEM((n * cap_pad // 2, positions), bf16),
            pltpu.VMEM((n, LANES), jnp.int32),
            pltpu.VMEM((n, LANES), jnp.int32),
            pltpu.VMEM((KV_HEADS, 1, positions), f32),
            pltpu.VMEM((16 * KV_HEADS, LANES), f32),
            pltpu.VMEM((n, 1, LANES), f32),
            pltpu.VMEM((n, 1, LANES), f32),
            pltpu.SMEM((1,), jnp.int32),
            pltpu.VMEM((slots,), jnp.int32),
            pltpu.VMEM((slots,), jnp.int32),
        ]
        + [dma((KV_HEADS,))] * 8
        + [dma((KV_HEADS,)), dma((1,)), dma((1,)), dma((KV_HEADS,)), dma((1,)), dma((1,))]
        + [dma((2,)), dma((2,)), dma((1,)), dma((1,)), dma((7,)), dma((1,)), dma((1,))],
        compiler_params=pltpu.CompilerParams(
            collective_id=0, has_side_effects=True, vmem_limit_bytes=60 * 1024 * 1024
        ),
        name="snap",
    )(cached_keys, cached_values, wq, kept_count, kept_entry, row_owner)
    importance, rows, score = pl.pallas_call(
        functools.partial(finish, cap),
        out_shape=(
            jax.ShapeDtypeStruct((KV_HEADS, positions), f32),
            jax.ShapeDtypeStruct((n, cap, 2 * HEAD_DIM), bf16),
            jax.ShapeDtypeStruct((n * cap,), bf16),
        ),
        in_specs=[vmem, vmem, vmem],
        out_specs=(vmem, vmem, vmem),
        name="finish",
    )(importance, rows, score)
    return importance, rows.reshape(n * cap, 2 * HEAD_DIM), score


def solution(mesh):
    n = mesh.shape["seq"]
    split = P(("rep", "seq"))
    wide = P(("rep", "seq"), None)
    return jax.shard_map(
        functools.partial(per_device, n),
        mesh=mesh,
        in_specs=(wide, wide, wide, split, split, split),
        out_specs=(P("rep", "seq"), wide, split),
        check_vma=False,
    )
```

```python
import functools

import jax
import jax.numpy as jnp
from jax import lax
from jax.experimental import pallas as pl
from jax.experimental.pallas import tpu as pltpu
from jax.sharding import PartitionSpec as P

KV_HEADS = 8
GROUP = 8
HEAD_DIM = 128
POOL = 7
LOG2E = 1.4426950408889634
LANES = 128
EDGE = 16
STRIP = 64
MESH = pl.DeviceIdType.MESH
NT = (((1,), (1,)), ((), ()))


def iota(shape, dim):
    return lax.broadcasted_iota(jnp.int32, shape, dim)


def kernel(
    n, cap, cap_pad, pool_scale,
    keys_hbm, vals_hbm, wq_hbm, count_hbm, entry_hbm, owner_hbm,
    imp_out, rows_out, score_out,
    keys, vals, qall, ebuf, raw, peak, sums, stat, stat_in, stat_all, glob, rows_send, onehot, slot_tile, slot_lane,
    mass, edge, ssend, imp_ref, count_ref, entry_ref, owner_ref,
    zs, zr, ws, wr, ys, yr, bs, br, ts, tr, gs, gr, rs, rr, hs, hr, ss, sr, ls, es, er,
):
    G = KV_HEADS
    me = lax.axis_index("seq")
    A = n // 4
    A1 = A // 2
    a, b, c = me // 4, (me // 2) % 2, me % 2
    a1, a0 = a // 2, a % 2
    slots = entry_ref.shape[0]
    positions = vals.shape[0]
    tiles = positions // LANES
    out_slots = n * cap_pad
    queries = ebuf.shape[2]
    scale2 = HEAD_DIM ** (-0.5) * LOG2E
    per_owner = n // G

    def stat_owner(g):
        return (g * per_owner + n // 2) % n

    def to(index):
        return {"seq": index}

    def remote(src, dst, ssem, rsem, index):
        return pltpu.make_async_remote_copy(
            src_ref=src, dst_ref=dst, send_sem=ssem, recv_sem=rsem,
            device_id=to(index), device_id_type=MESH,
        )

    def drain(region, sem):
        pltpu.make_async_copy(region, region, sem).wait()

    barrier = pltpu.get_barrier_semaphore()

    @pl.loop(1, n)
    def _(k):
        pl.semaphore_signal(barrier, inc=1, device_id=to(lax.rem(me + k, n)), device_id_type=MESH)

    own_q = pltpu.make_async_copy(wq_hbm, qall.at[:, c, b, a0, a1], ls.at[2])
    small = [
        pltpu.make_async_copy(src, dst, ls.at[4 + i])
        for i, (src, dst) in enumerate(((count_hbm, count_ref), (entry_hbm, entry_ref), (owner_hbm, owner_ref)))
    ]
    key_copy = pltpu.make_async_copy(keys_hbm, keys.at[pl.ds(0, positions)], ls.at[0])
    val_copy = pltpu.make_async_copy(vals_hbm, vals, ls.at[1])
    own_q.start()
    for copy in small:
        copy.start()
    key_copy.start()
    val_copy.start()

    low, high = lax.rem(me + n - 1, n), lax.rem(me + 1, n)
    mid_peer = a * 4 + (1 - b) * 2 + c
    core_peer = a * 4 + b * 2 + (1 - c)
    step_peer = (a + 1 - 2 * a0) * 4 + b * 2 + c
    first_rows = pl.ds(0, EDGE)
    last_rows = pl.ds(positions - EDGE, EDGE)
    from_low = pl.ds(positions, EDGE)
    from_high = pl.ds(positions + EDGE, EDGE)

    @pl.when(me == 0)
    def _():
        keys[positions:positions + EDGE, :] = jnp.zeros((EDGE, keys.shape[1]), keys.dtype)

    @pl.when(me == n - 1)
    def _():
        keys[positions + EDGE:positions + 2 * EDGE, :] = jnp.zeros((EDGE, keys.shape[1]), keys.dtype)

    def send_own(g):
        mine, place = wq_hbm.at[g], qall.at[g, c, b, a0, a1]

        @pl.loop(1, A1)
        def _(k):
            peer = (lax.rem(a1 + k, A1) * 2 + a0) * 4 + b * 2 + c
            remote(mine, place, zs.at[g], zr.at[g], peer).start()

        remote(mine, place, ys.at[g], yr.at[g], mid_peer).start()

    ahead = 3

    def greet():
        pl.semaphore_wait(barrier, n - 1)

        @pl.loop(0, ahead)
        def _(g):
            send_own(g)

        @pl.when(me > 0)
        def _():
            remote(keys_hbm.at[first_rows], keys.at[from_high], hs.at[0], hr.at[0], low).start()

        @pl.when(me < n - 1)
        def _():
            remote(keys_hbm.at[last_rows], keys.at[from_low], hs.at[1], hr.at[1], high).start()

    late = me >= n // 2

    @pl.when(late)
    def _():
        greet()

    for copy in small:
        copy.wait()
    entry = entry_ref[...].reshape(1, slots)
    owner = owner_ref[...].reshape(1, slots)
    live = iota((1, slots), 1) < count_ref[0]
    owner_live = jnp.where(live, owner, -1)
    member = jnp.where(iota((n, slots), 0) == owner_live, 1.0, 0.0)
    before = jnp.where(iota((slots, slots), 0) < iota((slots, slots), 1), 1.0, 0.0).astype(jnp.bfloat16)
    earlier = jnp.dot(member.astype(jnp.bfloat16), before, preferred_element_type=jnp.float32)
    rank = jnp.sum(member * earlier, axis=0, keepdims=True).astype(jnp.int32)
    target = jnp.where(live, owner * cap_pad + rank, -1)
    tile_of = entry // LANES
    lane_of = entry - tile_of * LANES
    head = tile_of // tiles
    token_f = (entry - head * positions + 1).astype(jnp.float32)
    head_f = head.astype(jnp.float32)
    at_rank = jnp.where(iota((LANES, slots), 0) == rank, 1.0, 0.0).astype(jnp.bfloat16)

    def by_rank(value):
        marked = (member * value.astype(jnp.float32)).astype(jnp.bfloat16)
        return lax.dot_general(marked, at_rank, NT, preferred_element_type=jnp.float32).astype(jnp.int32)

    slot_tile[...] = by_rank(tile_of + 1)
    slot_lane[...] = by_rank(lane_of)

    @pl.when(jnp.logical_not(late))
    def _():
        greet()

    key_copy.wait()
    val_copy.wait()

    def gather_rows(k0, count):
        blk = count * cap_pad
        hit = (iota((blk, slots), 0) + k0 * cap_pad) == target
        tok = jnp.sum(jnp.where(hit, token_f, 0.0), axis=1, keepdims=True).astype(jnp.int32) - 1
        hcol = jnp.sum(jnp.where(hit, head_f, 0.0), axis=1, keepdims=True).astype(jnp.int32)
        hcol = jnp.broadcast_to(hcol, (blk, HEAD_DIM))
        onehot[...] = jnp.where(iota((blk, positions), 1) == tok, 1.0, 0.0).astype(jnp.bfloat16)
        for side, source in enumerate((keys, vals)):
            got = jnp.dot(onehot[...], source[0:positions, :], preferred_element_type=jnp.float32)
            chosen = jnp.zeros((blk, HEAD_DIM), jnp.float32)
            for h in range(G):
                chosen = jnp.where(hcol == h, got[:, h * HEAD_DIM:(h + 1) * HEAD_DIM], chosen)
            for k in range(count):
                rows_send[k0 + k, :, side * HEAD_DIM:(side + 1) * HEAD_DIM] = chosen[
                    k * cap_pad:(k + 1) * cap_pad
                ].astype(jnp.bfloat16)

    per = onehot.shape[0] // cap_pad
    for i in range(n // per):
        gather_rows(i * per, per)

    def lse(values):
        top = values[0]
        for x in values[1:]:
            top = jnp.maximum(top, x)
        total = jnp.zeros_like(top)
        for x in values:
            total = total + jnp.exp2(x - top)
        return top + jnp.log(total) * LOG2E

    def join(g, gathered):
        gathered[me] = stat[g]
        glob[g] = lse([gathered[d] for d in range(n)])

    def combine(g):
        @pl.when(me == stat_owner(g))
        def _():
            drain(stat_in.at[pl.ds(0, n - 1)], tr.at[0])
            join(g, stat_in)

            @pl.loop(1, n)
            def _(k):
                remote(glob.at[g], glob.at[g], gs.at[0], gr.at[g], lax.rem(me + k, n)).start()

    chunk = 2 * LANES
    strip = sums.shape[0]
    span = positions // strip

    def compute(g):
        group_q = qall.at[g].reshape(queries, HEAD_DIM)
        key_cols = pl.ds(pl.multiple_of(g * HEAD_DIM, HEAD_DIM), HEAD_DIM)
        for j in range(queries // chunk):
            lanes = slice(j * chunk, (j + 1) * chunk)
            s = lax.dot_general(
                keys[:, key_cols], group_q[lanes, :], NT, preferred_element_type=jnp.float32
            )
            for u in range(strip):
                x = s[u * span:(u + 1) * span].reshape(span // 8, 8, chunk)
                top = jnp.max(x, axis=0)
                e = jnp.exp2((x - top[None]) * scale2)
                ebuf[g, u * span:(u + 1) * span, lanes] = e.reshape(span, chunk)
                peak[g, u, :, lanes] = top
                sums[u, :, lanes] = jnp.sum(e, axis=0)
            raw[g, 0:8, lanes] = s[positions + EDGE - 8:positions + EDGE]
            raw[g, 8:16, lanes] = s[positions + EDGE:positions + EDGE + 8]
        tops = peak[g]
        top = jnp.max(jnp.max(tops, axis=0), axis=0, keepdims=True)
        total = jnp.sum(jnp.sum(sums[...] * jnp.exp2((tops - top[None]) * scale2), axis=0), axis=0, keepdims=True)
        local = top * scale2 + jnp.log(total) * LOG2E
        for i in range(queries // LANES):
            stat[g, i:i + 1, :] = local[:, i * LANES:(i + 1) * LANES]

        dest = stat_owner(g)

        @pl.when((g < G - 1) & (me != dest))
        def _():
            remote(stat.at[g], stat_in.at[me], ts.at[g], tr.at[0], dest).start()

        @pl.when(g == G - 1)
        def _():
            @pl.loop(1, n)
            def _(k):
                remote(stat.at[g], stat_all.at[me], es.at[0], er.at[0], lax.rem(me + k, n)).start()

    own_rows = pltpu.make_async_copy(rows_send.at[me], rows_out.at[me], ls.at[3])
    own_rows.start()
    own_q.wait()
    first, bunch = 4, -(-n // G)

    lag = 8

    @pl.loop(0, G + 5)
    def _(step):
        @pl.when(step < G)
        def _():
            g = step

            @pl.when(g < G - ahead)
            def _():
                send_own(g + ahead)

            drain(qall.at[g, c, b, a0, pl.ds(0, A1 - 1)], zr.at[g])
            mine = qall.at[g, c, b, a0]
            remote(mine, mine, ws.at[g], wr.at[g], step_peer).start()

            @pl.loop(1, A1)
            def _(k):
                other = qall.at[g, c, b, a0, lax.rem(a1 + k, A1)]
                remote(other, other, ys.at[g], yr.at[g], mid_peer).start()

        @pl.when((step >= 2) & (step < G + 2))
        def _():
            g = step - 2
            drain(qall.at[g, c, b, 1 - a0], wr.at[g])
            other = qall.at[g, c, b, 1 - a0]
            remote(other, other, ys.at[g], yr.at[g], mid_peer).start()

        @pl.when((step >= 4) & (step < G + 4))
        def _():
            g = step - 4
            drain(qall.at[g, c, 1 - b], yr.at[g])
            remote(qall.at[g, c], qall.at[g, c], bs.at[g], br.at[g], core_peer).start()

        @pl.when((step >= first) & (step < first + G))
        def _():
            @pl.loop(0, bunch)
            def _(i):
                k = (step - first) * bunch + i

                @pl.when((k > 0) & (k < n))
                def _():
                    peer = lax.rem(me + k, n)
                    remote(rows_send.at[peer], rows_out.at[me], rs.at[0], rr.at[0], peer).start()

        @pl.when((step == 5) & (me < n - 1))
        def _():
            drain(keys.at[from_high], hr.at[0])

        @pl.when((step == 5) & (me > 0))
        def _():
            drain(keys.at[from_low], hr.at[1])

        @pl.when(step >= 5)
        def _():
            g = step - 5
            drain(qall.at[g, 1 - c], br.at[g])
            compute(g)

        @pl.when(step >= lag)
        def _():
            combine(step - lag)

    @pl.loop(G + 5 - lag, G - 1)
    def _(g):
        combine(g)

    @pl.loop(0, G)
    def _(g):
        @pl.when((g < G - 1) & (me != stat_owner(g)))
        def _():
            drain(glob.at[g], gr.at[g])

        @pl.when(g == G - 1)
        def _():
            drain(stat_all.at[pl.ds(0, n - 1)], er.at[0])
            join(g, stat_all)

        whole = glob[g]
        level = [whole[k:k + 1, :] for k in range(queries // LANES)]

        def weighted(value, k):
            return value * weight[:, k * LANES:(k + 1) * LANES][None]

        for t in range(tiles):
            acc = None
            for u in range(t * LANES // span, max((t + 1) * LANES // span, t * LANES // span + 1)):
                weight = jnp.concatenate(
                    [
                        jnp.exp2(peak[g, u, :, k * LANES:(k + 1) * LANES] * scale2 - level[k])
                        for k in range(queries // LANES)
                    ],
                    axis=1,
                )
                r0 = max(u * span, t * LANES)
                rows = min(span, LANES)
                part = None
                for k in range(queries // LANES):
                    e = ebuf[g, r0:r0 + rows, k * LANES:(k + 1) * LANES].reshape(rows // 8, 8, LANES)
                    e = weighted(e, k)
                    part = e if part is None else part + e
                part = part.reshape(rows, LANES)
                acc = part if acc is None else jnp.concatenate([acc, part], axis=0)
            mass[g, :, t * LANES:(t + 1) * LANES] = jnp.sum(acc.T, axis=0, keepdims=True)
        acc = None
        for k in range(queries // LANES):
            e = jnp.exp2(raw[g, :, k * LANES:(k + 1) * LANES] * scale2 - level[k])
            acc = e if acc is None else acc + e
        edge[pl.ds(pl.multiple_of(g * 16, 16), 16), :] = acc

    column = jnp.concatenate([mass[g] for g in range(G)], axis=0)
    line = jnp.sum(edge[...].T, axis=0, keepdims=True)
    row_of = iota((G, LANES), 0)
    ends = jnp.zeros((G, LANES), jnp.float32)
    for g in range(G):
        turned = pltpu.roll(line, (LANES - 8 - 16 * g) % LANES, 1)
        ends = jnp.where(row_of == g, turned, ends)
    before_low = jnp.where(me > 0, ends, 0.0)
    after_high = jnp.where(me < n - 1, ends, 0.0)
    padded = jnp.concatenate([before_low, column, after_high], axis=1)
    width = padded.shape[1]
    pooled = padded
    for o in range(1, POOL // 2 + 1):
        pooled = pooled + pltpu.roll(padded, o, 1) + pltpu.roll(padded, width - o, 1)
    importance = pooled[:, LANES:LANES + positions] * pool_scale
    imp_ref[...] = importance
    own_imp = pltpu.make_async_copy(imp_ref, imp_out, ls.at[2])
    own_imp.start()

    want, lane = slot_tile[...], slot_lane[...]
    table = jnp.zeros((n, LANES), jnp.float32)
    for h in range(G):
        for t in range(tiles):
            part = jnp.broadcast_to(importance[h:h + 1, t * LANES:(t + 1) * LANES], (n, LANES))
            found = jnp.take_along_axis(part, lane, axis=1)
            table = jnp.where(want == h * tiles + t + 1, found, table)
    for k in range(n):
        ssend[k] = table[k:k + 1, :]
    own_score = pltpu.make_async_copy(ssend.at[me], score_out.at[me], ls.at[0])
    own_score.start()

    @pl.loop(1, n)
    def _(k):
        peer = lax.rem(me + k, n)
        remote(ssend.at[peer], score_out.at[me], ss.at[0], sr.at[0], peer).start()

    own_rows.wait()
    drain(rows_out.at[pl.ds(0, n - 1)], rr.at[0])
    drain(rows_send.at[pl.ds(0, n - 1)], rs.at[0])

    @pl.loop(0, G)
    def _(g):
        drain(qall.at[g, c, b, a0, pl.ds(0, A1 - 1)], zs.at[g])
        drain(qall.at[g, c, b, a0], ws.at[g])
        drain(qall.at[g, c, b], ys.at[g])
        drain(qall.at[g, c], bs.at[g])

        @pl.when((g < G - 1) & (me != stat_owner(g)))
        def _():
            drain(stat.at[g], ts.at[g])

        @pl.when((g < G - 1) & (me == stat_owner(g)))
        def _():
            drain(stat_in.at[pl.ds(0, n - 1)], gs.at[0])

    @pl.when(me > 0)
    def _():
        drain(keys.at[from_high], hs.at[0])

    @pl.when(me < n - 1)
    def _():
        drain(keys.at[from_low], hs.at[1])

    drain(stat_all.at[pl.ds(0, n - 1)], es.at[0])
    drain(ssend.at[pl.ds(0, n - 1)], ss.at[0])
    own_imp.wait()
    own_score.wait()
    drain(score_out.at[pl.ds(0, n - 1)], sr.at[0])


def finish(cap, imp_in, rows_in, score_in, imp_ref, rows_ref, score_ref):
    n = rows_in.shape[0]
    imp_ref[...] = imp_in[...]
    rows_ref[...] = rows_in[:, 0:cap, :]
    table = jnp.concatenate([score_in[k] for k in range(n)], axis=0).astype(jnp.bfloat16)
    column = iota((LANES, n * cap), 1) - iota((LANES, n * cap), 0)
    unfold = jnp.where(column % cap == 0, 1.0, 0.0)
    unfold = jnp.where(iota((LANES, n * cap), 0) < cap, unfold, 0.0).astype(jnp.bfloat16)
    wide = jnp.dot(table, unfold, preferred_element_type=jnp.float32)
    within = iota((n, n * cap), 1) - iota((n, n * cap), 0) * cap
    line = jnp.sum(jnp.where((within >= 0) & (within < cap), wide, 0.0), axis=0, keepdims=True)
    score_ref[...] = line.astype(jnp.bfloat16).reshape(n * cap)


def per_device(n, cached_keys, cached_values, window_queries, kept_count, kept_entry, row_owner):
    positions, width = cached_keys.shape
    slots = kept_entry.shape[0]
    cap = slots // n
    cap_pad = -(-cap // 8) * 8
    query_rows = window_queries.shape[0]
    heads = window_queries.shape[1] // HEAD_DIM
    group = heads // KV_HEADS
    window = query_rows * n
    qrows = query_rows * group
    lane_rows = n * qrows // LANES
    wq = (
        window_queries.reshape(query_rows, heads, HEAD_DIM)
        .transpose(1, 0, 2)
        .reshape(KV_HEADS, qrows, HEAD_DIM)
    )
    pool_scale = n * positions / (group * window * POOL)
    any_spec = pl.BlockSpec(memory_space=pl.ANY)
    vmem = pl.BlockSpec(memory_space=pltpu.VMEM)
    dma = pltpu.SemaphoreType.DMA
    A = n // 4
    f32, bf16 = jnp.float32, jnp.bfloat16
    importance, rows, score = pl.pallas_call(
        functools.partial(kernel, n, cap, cap_pad, pool_scale),
        out_shape=(
            jax.ShapeDtypeStruct((KV_HEADS, positions), f32),
            jax.ShapeDtypeStruct((n, cap_pad, 2 * HEAD_DIM), bf16),
            jax.ShapeDtypeStruct((n, 1, LANES), f32),
        ),
        in_specs=[any_spec] * 6,
        out_specs=(any_spec, any_spec, any_spec),
        scratch_shapes=[
            pltpu.VMEM((positions + 2 * EDGE, width), bf16),
            pltpu.VMEM((positions, width), bf16),
            pltpu.VMEM((KV_HEADS, 2, 2, 2, A // 2, qrows, HEAD_DIM), bf16),
            pltpu.VMEM((KV_HEADS, positions, n * qrows), f32),
            pltpu.VMEM((KV_HEADS, 16, n * qrows), f32),
            pltpu.VMEM((KV_HEADS, positions // STRIP, 8, n * qrows), f32),
            pltpu.VMEM((positions // STRIP, 8, n * qrows), f32),
            pltpu.VMEM((KV_HEADS, lane_rows, LANES), f32),
            pltpu.VMEM((n, lane_rows, LANES), f32),
            pltpu.VMEM((n, lane_rows, LANES), f32),
            pltpu.VMEM((KV_HEADS, lane_rows, LANES), f32),
            pltpu.VMEM((n, cap_pad, 2 * HEAD_DIM), bf16),
            pltpu.VMEM((n * cap_pad // 2, positions), bf16),
            pltpu.VMEM((n, LANES), jnp.int32),
            pltpu.VMEM((n, LANES), jnp.int32),
            pltpu.VMEM((KV_HEADS, 1, positions), f32),
            pltpu.VMEM((16 * KV_HEADS, LANES), f32),
            pltpu.VMEM((n, 1, LANES), f32),
            pltpu.VMEM((KV_HEADS, positions), f32),
            pltpu.SMEM((1,), jnp.int32),
            pltpu.VMEM((slots,), jnp.int32),
            pltpu.VMEM((slots,), jnp.int32),
        ]
        + [dma((KV_HEADS,))] * 8
        + [dma((KV_HEADS,)), dma((1,)), dma((1,)), dma((KV_HEADS,)), dma((1,)), dma((1,))]
        + [dma((2,)), dma((2,)), dma((1,)), dma((1,)), dma((7,)), dma((1,)), dma((1,))],
        compiler_params=pltpu.CompilerParams(
            collective_id=0, has_side_effects=True, vmem_limit_bytes=60 * 1024 * 1024
        ),
        name="snap",
    )(cached_keys, cached_values, wq, kept_count, kept_entry, row_owner)
    importance, rows, score = pl.pallas_call(
        functools.partial(finish, cap),
        out_shape=(
            jax.ShapeDtypeStruct((KV_HEADS, positions), f32),
            jax.ShapeDtypeStruct((n, cap, 2 * HEAD_DIM), bf16),
            jax.ShapeDtypeStruct((n * cap,), bf16),
        ),
        in_specs=[vmem, vmem, vmem],
        out_specs=(vmem, vmem, vmem),
        name="finish",
    )(importance, rows, score)
    return importance, rows.reshape(n * cap, 2 * HEAD_DIM), score


def solution(mesh):
    n = mesh.shape["seq"]
    split = P(("rep", "seq"))
    wide = P(("rep", "seq"), None)
    return jax.shard_map(
        functools.partial(per_device, n),
        mesh=mesh,
        in_specs=(wide, wide, wide, split, split, split),
        out_specs=(P("rep", "seq"), wide, split),
        check_vma=False,
    )
```

```python
import functools

import jax
import jax.numpy as jnp
from jax import lax
from jax.experimental import pallas as pl
from jax.experimental.pallas import tpu as pltpu
from jax.sharding import PartitionSpec as P

KV_HEADS = 8
GROUP = 8
HEAD_DIM = 128
POOL = 7
LOG2E = 1.4426950408889634
LANES = 128
EDGE = 16
STRIP = 64
HALVES = 2
MESH = pl.DeviceIdType.MESH
NT = (((1,), (1,)), ((), ()))


def iota(shape, dim):
    return lax.broadcasted_iota(jnp.int32, shape, dim)


def kernel(
    n, cap, cap_pad, pool_scale,
    keys_hbm, vals_hbm, wq_hbm, count_hbm, entry_hbm, owner_hbm,
    imp_out, rows_out, score_out,
    keys, vals, qall, ebuf, raw, peak, sums, macc, stat, stat_x, stat_z, rows_send, onehot, slot_tile, slot_lane,
    mass, edge, ssend, imp_ref, count_ref, entry_ref, owner_ref,
    zs, zr, ws, wr, ys, yr, bs, br, xs, xr, qs, qr, rs, rr, hs, hr, ss, sr, ls,
):
    G = KV_HEADS
    me = lax.axis_index("seq")
    A = n // 4
    N, U = qall.shape[1], qall.shape[4]
    H = G // HALVES
    units = N * HALVES
    relay = U == 1 and N == 4
    a, b, c = me // 4, (me // 2) % 2, me % 2
    inner = a % U

    mine = a // U
    slots = entry_ref.shape[0]
    positions = vals.shape[0]
    tiles = positions // LANES
    out_slots = n * cap_pad
    chunk = ebuf.shape[3]
    scale2 = HEAD_DIM ** (-0.5) * LOG2E
    quad = b * 2 + c

    def to(index):
        return {"seq": index}

    def remote(src, dst, ssem, rsem, index):
        return pltpu.make_async_remote_copy(
            src_ref=src, dst_ref=dst, send_sem=ssem, recv_sem=rsem,
            device_id=to(index), device_id_type=MESH,
        )

    def drain(region, sem):
        pltpu.make_async_copy(region, region, sem).wait()

    low, high = lax.rem(me + n - 1, n), lax.rem(me + 1, n)
    mid_peer = a * 4 + (1 - b) * 2 + c
    core_peer = a * 4 + b * 2 + (1 - c)
    near, across = a + 1 - 2 * (a % 2), (a + 2) % A

    def hop_of(p):
        return jnp.where(a < 2, jnp.where(p == 0, 0, jnp.where(p == 3, 1, p + 1)), p)

    def unit_at(p):
        if not relay:
            return lax.rem(mine + p, N)
        hop = hop_of(p)
        return jnp.where(hop == 0, a, jnp.where(hop == 1, near, jnp.where(hop == 2, across, A - 1 - a)))

    def joined_at(p):
        return jnp.where(p < 2, p + 2, 3 - p) if relay else p


    def line_peer(k):
        return lax.rem(a + k, A) * 4 + b * 2 + c

    barrier = pltpu.get_barrier_semaphore()

    def announce(index):
        pl.semaphore_signal(barrier, inc=1, device_id=to(index), device_id_type=MESH)

    @pl.loop(1, A)
    def _(k):
        announce(line_peer(k))

    announce(mid_peer)
    announce(core_peer)

    @pl.when(me > 0)
    def _():
        announce(low)

    @pl.when(me < n - 1)
    def _():
        announce(high)

    own_q = pltpu.make_async_copy(wq_hbm, qall.at[:, mine, c, b, inner], ls.at[2])
    small = [
        pltpu.make_async_copy(src, dst, ls.at[4 + i])
        for i, (src, dst) in enumerate(((count_hbm, count_ref), (entry_hbm, entry_ref), (owner_hbm, owner_ref)))
    ]
    key_copy = pltpu.make_async_copy(keys_hbm, keys.at[pl.ds(0, positions)], ls.at[0])
    val_copy = pltpu.make_async_copy(vals_hbm, vals, ls.at[1])
    own_q.start()
    for copy in small:
        copy.start()
    key_copy.start()
    val_copy.start()

    first_rows = pl.ds(0, EDGE)
    last_rows = pl.ds(positions - EDGE, EDGE)
    from_low = pl.ds(positions, EDGE)
    from_high = pl.ds(positions + EDGE, EDGE)

    @pl.when(me == 0)
    def _():
        keys[positions:positions + EDGE, :] = jnp.zeros((EDGE, keys.shape[1]), keys.dtype)

    @pl.when(me == n - 1)
    def _():
        keys[positions + EDGE:positions + 2 * EDGE, :] = jnp.zeros((EDGE, keys.shape[1]), keys.dtype)

    def half(h):
        return pl.ds(h * H, H)

    def pieces(count):
        return qall.at[half(0)].reshape(H * N * 4 * U, qall.shape[5], HEAD_DIM).at[pl.ds(0, H * count)]

    def on_line(index):
        return index * 4 + b * 2 + c

    def greet():
        ends = jnp.where(me > 0, 1, 0) + jnp.where(me < n - 1, 1, 0)
        pl.semaphore_wait(barrier, A + 1 + ends)

        @pl.loop(0, HALVES)
        def _(h):
            piece, place, k = wq_hbm.at[half(h)], qall.at[half(h), mine, c, b, inner], mine * HALVES + h

            def send(index):
                remote(piece, place, zs.at[h], zr.at[k], on_line(index)).start()

            if relay:
                send(near)
                send(across)
            else:
                @pl.loop(1, A)
                def _(i):
                    send(lax.rem(a + i, A))

        own_q.wait()
        if U == 1:
            @pl.loop(0, HALVES)
            def _(h):
                block = qall.at[half(h), mine, c, b]
                remote(block, block, ys.at[mine * HALVES + h], yr.at[mine * HALVES + h], mid_peer).start()

        @pl.when(me > 0)
        def _():
            remote(keys_hbm.at[first_rows], keys.at[from_high], hs.at[0], hr.at[0], low).start()

        @pl.when(me < n - 1)
        def _():
            remote(keys_hbm.at[last_rows], keys.at[from_low], hs.at[1], hr.at[1], high).start()

    reach = a + b
    late = reach > A // 2

    @pl.when(late)
    def _():
        greet()

    for copy in small:
        copy.wait()
    entry = entry_ref[...].reshape(1, slots)
    owner = owner_ref[...].reshape(1, slots)
    live = iota((1, slots), 1) < count_ref[0]
    owner_live = jnp.where(live, owner, -1)
    member = jnp.where(iota((n, slots), 0) == owner_live, 1.0, 0.0)
    before = jnp.where(iota((slots, slots), 0) < iota((slots, slots), 1), 1.0, 0.0).astype(jnp.bfloat16)
    earlier = jnp.dot(member.astype(jnp.bfloat16), before, preferred_element_type=jnp.float32)
    rank = jnp.sum(member * earlier, axis=0, keepdims=True).astype(jnp.int32)
    target = jnp.where(live, owner * cap_pad + rank, -1)
    tile_of = entry // LANES
    lane_of = entry - tile_of * LANES
    head = tile_of // tiles
    token_f = (entry - head * positions + 1).astype(jnp.float32)
    head_f = head.astype(jnp.float32)
    at_rank = jnp.where(iota((LANES, slots), 0) == rank, 1.0, 0.0).astype(jnp.bfloat16)

    def by_rank(value):
        marked = (member * value.astype(jnp.float32)).astype(jnp.bfloat16)
        return lax.dot_general(marked, at_rank, NT, preferred_element_type=jnp.float32).astype(jnp.int32)

    slot_tile[...] = by_rank(tile_of + 1)
    slot_lane[...] = by_rank(lane_of)

    @pl.when(reach == A // 2)
    def _():
        greet()

    key_copy.wait()
    val_copy.wait()

    def gather_rows(k0, count):
        blk = count * cap_pad
        hit = (iota((blk, slots), 0) + k0 * cap_pad) == target
        tok = jnp.sum(jnp.where(hit, token_f, 0.0), axis=1, keepdims=True).astype(jnp.int32) - 1
        hcol = jnp.sum(jnp.where(hit, head_f, 0.0), axis=1, keepdims=True).astype(jnp.int32)
        hcol = jnp.broadcast_to(hcol, (blk, HEAD_DIM))
        onehot[...] = jnp.where(iota((blk, positions), 1) == tok, 1.0, 0.0).astype(jnp.bfloat16)
        for side, source in enumerate((keys, vals)):
            got = jnp.dot(onehot[...], source[0:positions, :], preferred_element_type=jnp.float32)
            chosen = jnp.zeros((blk, HEAD_DIM), jnp.float32)
            for h in range(G):
                chosen = jnp.where(hcol == h, got[:, h * HEAD_DIM:(h + 1) * HEAD_DIM], chosen)
            for k in range(count):
                rows_send[k0 + k, :, side * HEAD_DIM:(side + 1) * HEAD_DIM] = chosen[
                    k * cap_pad:(k + 1) * cap_pad
                ].astype(jnp.bfloat16)

    per = onehot.shape[0] // cap_pad
    gather_rows(0, per)

    @pl.when(reach < A // 2)
    def _():
        greet()

    def lse(values):
        top = values[0]
        for x in values[1:]:
            top = jnp.maximum(top, x)
        total = jnp.zeros_like(top)
        for x in values:
            total = total + jnp.exp2(x - top)
        return top + jnp.log(total) * LOG2E

    def join_quad(i):
        g = unit_at(i // HALVES) * HALVES + i % HALVES
        drain(stat_x.at[g, pl.ds(0, 3)], xr.at[g])
        stat_z[g, a] = lse([stat_x[g, d] for d in range(4)])

        @pl.loop(1, A)
        def _(k):
            peer = lax.rem(a + k, A) * 4 + quad
            remote(stat_z.at[g, a], stat_z.at[g, a], qs.at[g], qr.at[g], peer).start()

    strip = sums.shape[1]
    span = positions // strip
    columns = chunk // LANES

    def compute(r, h):
        k = r * HALVES + h
        for i in range(H):
            g = h * H + i
            group_q = qall.at[g, r].reshape(chunk, HEAD_DIM)
            key_cols = pl.ds(pl.multiple_of(g * HEAD_DIM, HEAD_DIM), HEAD_DIM)
            s = lax.dot_general(keys[:, key_cols], group_q[...], NT, preferred_element_type=jnp.float32)
            for u in range(strip):
                x = s[u * span:(u + 1) * span].reshape(span // 8, 8, chunk)
                top = jnp.max(x, axis=0)
                e = jnp.exp2((x - top[None]) * scale2)
                ebuf[k, i, u * span:(u + 1) * span, :] = e.reshape(span, chunk)
                peak[k, i, u] = top
                sums[i, u] = jnp.sum(e, axis=0)
            raw[k, i, 0:8, :] = s[positions + EDGE - 8:positions + EDGE]
            raw[k, i, 8:16, :] = s[positions + EDGE:positions + EDGE + 8]
        for i in range(H):
            tops = peak[k, i]
            top = jnp.max(jnp.max(tops, axis=0), axis=0, keepdims=True)
            total = jnp.sum(jnp.sum(sums[i] * jnp.exp2((tops - top[None]) * scale2), axis=0), axis=0, keepdims=True)
            local = top * scale2 + jnp.log(total) * LOG2E
            for j in range(columns):
                stat[k, i * columns + j:i * columns + j + 1, :] = local[:, j * LANES:(j + 1) * LANES]
        stat_x[k, quad] = stat[k]

        @pl.loop(1, 4)
        def _(d):
            peer = a * 4 + lax.rem(quad + d, 4)
            remote(stat.at[k], stat_x.at[k, quad], xs.at[k], xr.at[k], peer).start()

    own_rows = pltpu.make_async_copy(rows_send.at[me], rows_out.at[me], ls.at[3])
    lag = 3

    @pl.loop(0, G)
    def _(g):
        macc[g] = jnp.zeros(macc.shape[1:], jnp.float32)

    edge[...] = jnp.zeros(edge.shape, jnp.float32)

    def send_middle(i):
        p, h = i // HALVES, i % HALVES
        unit = unit_at(p)
        k = unit * HALVES + h
        block = qall.at[half(h), unit, c, b]

        @pl.when(p > 0)
        def _():
            drain(pieces(U), zr.at[k])

        if U > 1:
            @pl.when(p == 0)
            def _():
                drain(pieces(U - 1), zr.at[k])

            remote(block, block, ys.at[k], yr.at[k], mid_peer).start()
        else:
            @pl.when(p > 0)
            def _():
                remote(block, block, ys.at[k], yr.at[k], mid_peer).start()

        if relay:
            @pl.when(hop_of(p) == 2)
            def _():
                remote(block, block, ws.at[h], zr.at[k], on_line(near)).start()

    def send_core(i):
        h = i % HALVES
        unit = unit_at(i // HALVES)
        k = unit * HALVES + h
        drain(qall.at[half(h), unit, c, 1 - b], yr.at[k])
        block = qall.at[half(h), unit, c]
        remote(block, block, bs.at[k], br.at[k], core_peer).start()

    if U > 1:
        for i in range(HALVES):
            send_middle(i)

    @pl.loop(0, units + 1)
    def _(step):
        @pl.when((step > 0) & (step < units - 2))
        def _():
            send_middle(step + 2)

        @pl.when(step < units)
        def _():
            send_core(step)

        @pl.when(step == 0)
        def _():
            gather_rows(per, per)
            own_rows.start()
            send_middle(step + 2)

        @pl.when((step == 1) & (me < n - 1))
        def _():
            drain(keys.at[from_high], hr.at[0])

        @pl.when((step == 1) & (me > 0))
        def _():
            drain(keys.at[from_low], hr.at[1])

        @pl.when(step >= 1)
        def _():
            h = (step - 1) % HALVES
            unit = unit_at((step - 1) // HALVES)
            drain(qall.at[half(h), unit, 1 - c], br.at[unit * HALVES + h])
            compute(unit, h)

        @pl.when(step >= lag)
        def _():
            join_quad(step - lag)

    join_quad(units - 2)
    join_quad(units - 1)

    @pl.loop(1, n)
    def _(k):
        peer = lax.rem(me + k, n)
        remote(rows_send.at[peer], rows_out.at[me], rs.at[0], rr.at[0], peer).start()

    @pl.loop(0, units)
    def _(i):
        h = i % HALVES
        k = joined_at(i // HALVES) * HALVES + h
        drain(stat_z.at[k, pl.ds(0, A - 1)], qr.at[k])
        whole = lse([stat_z[k, d] for d in range(A)])
        for j in range(H):
            g = h * H + j
            level = [whole[j * columns + d:j * columns + d + 1, :] for d in range(columns)]
            for u in range(strip):
                weight = [
                    jnp.exp2(peak[k, j, u, :, d * LANES:(d + 1) * LANES] * scale2 - level[d]) for d in range(columns)
                ]
                rows = slice(u * span, (u + 1) * span)
                acc = macc[g, rows, :].reshape(span // 8, 8, LANES)
                for d in range(columns):
                    e = ebuf[k, j, rows, d * LANES:(d + 1) * LANES].reshape(span // 8, 8, LANES)
                    acc = acc + e * weight[d][None]
                macc[g, rows, :] = acc.reshape(span, LANES)
            acc = edge[pl.ds(pl.multiple_of(g * 16, 16), 16), :]
            for d in range(columns):
                acc = acc + jnp.exp2(raw[k, j, :, d * LANES:(d + 1) * LANES] * scale2 - level[d])
            edge[pl.ds(pl.multiple_of(g * 16, 16), 16), :] = acc

        @pl.when(i >= units - HALVES)
        def _():
            for j in range(H):
                g = h * H + j
                for t in range(tiles):
                    acc = macc[g, t * LANES:(t + 1) * LANES, :]
                    mass[g, :, t * LANES:(t + 1) * LANES] = jnp.sum(acc.T, axis=0, keepdims=True)

    column = jnp.concatenate([mass[g] for g in range(G)], axis=0)
    line = jnp.sum(edge[...].T, axis=0, keepdims=True)
    row_of = iota((G, LANES), 0)
    ends = jnp.zeros((G, LANES), jnp.float32)
    for g in range(G):
        turned = pltpu.roll(line, (LANES - 8 - 16 * g) % LANES, 1)
        ends = jnp.where(row_of == g, turned, ends)
    before_low = jnp.where(me > 0, ends, 0.0)
    after_high = jnp.where(me < n - 1, ends, 0.0)
    padded = jnp.concatenate([before_low, column, after_high], axis=1)
    width = padded.shape[1]
    pooled = padded
    for o in range(1, POOL // 2 + 1):
        pooled = pooled + pltpu.roll(padded, o, 1) + pltpu.roll(padded, width - o, 1)
    importance = pooled[:, LANES:LANES + positions] * pool_scale
    imp_ref[...] = importance
    own_imp = pltpu.make_async_copy(imp_ref, imp_out, ls.at[2])
    own_imp.start()

    want, lane = slot_tile[...], slot_lane[...]
    table = jnp.zeros((n, LANES), jnp.float32)
    for h in range(G):
        for t in range(tiles):
            part = jnp.broadcast_to(importance[h:h + 1, t * LANES:(t + 1) * LANES], (n, LANES))
            found = jnp.take_along_axis(part, lane, axis=1)
            table = jnp.where(want == h * tiles + t + 1, found, table)
    for k in range(n):
        ssend[k] = table[k:k + 1, :]
    own_score = pltpu.make_async_copy(ssend.at[me], score_out.at[me], ls.at[0])
    own_score.start()

    @pl.loop(1, n)
    def _(k):
        peer = lax.rem(me + k, n)
        remote(ssend.at[peer], score_out.at[me], ss.at[0], sr.at[0], peer).start()

    own_rows.wait()
    drain(rows_out.at[pl.ds(0, n - 1)], rr.at[0])
    drain(rows_send.at[pl.ds(0, n - 1)], rs.at[0])

    @pl.loop(0, HALVES)
    def _(h):
        if relay:
            drain(pieces(2), zs.at[h])
            drain(pieces(1), ws.at[h])
        else:
            drain(pieces(A - 1), zs.at[h])

    @pl.loop(0, units)
    def _(k):
        r, h = k // HALVES, k % HALVES
        drain(qall.at[half(h), r, c, b], ys.at[k])
        drain(qall.at[half(h), r, c], bs.at[k])
        drain(stat_x.at[k, pl.ds(0, 3)], xs.at[k])
        drain(stat_z.at[k, pl.ds(0, A - 1)], qs.at[k])

    @pl.when(me > 0)
    def _():
        drain(keys.at[from_high], hs.at[0])

    @pl.when(me < n - 1)
    def _():
        drain(keys.at[from_low], hs.at[1])

    drain(ssend.at[pl.ds(0, n - 1)], ss.at[0])
    own_imp.wait()
    own_score.wait()
    drain(score_out.at[pl.ds(0, n - 1)], sr.at[0])


def finish(cap, imp_in, rows_in, score_in, imp_ref, rows_ref, score_ref):
    n = rows_in.shape[0]
    imp_ref[...] = imp_in[...]
    rows_ref[...] = rows_in[:, 0:cap, :]
    table = jnp.concatenate([score_in[k] for k in range(n)], axis=0).astype(jnp.bfloat16)
    column = iota((LANES, n * cap), 1) - iota((LANES, n * cap), 0)
    unfold = jnp.where(column % cap == 0, 1.0, 0.0)
    unfold = jnp.where(iota((LANES, n * cap), 0) < cap, unfold, 0.0).astype(jnp.bfloat16)
    wide = jnp.dot(table, unfold, preferred_element_type=jnp.float32)
    within = iota((n, n * cap), 1) - iota((n, n * cap), 0) * cap
    line = jnp.sum(jnp.where((within >= 0) & (within < cap), wide, 0.0), axis=0, keepdims=True)
    score_ref[...] = line.astype(jnp.bfloat16).reshape(n * cap)


def per_device(n, cached_keys, cached_values, window_queries, kept_count, kept_entry, row_owner):
    positions, width = cached_keys.shape
    slots = kept_entry.shape[0]
    cap = slots // n
    cap_pad = -(-cap // 8) * 8
    query_rows = window_queries.shape[0]
    heads = window_queries.shape[1] // HEAD_DIM
    group = heads // KV_HEADS
    window = query_rows * n
    qrows = query_rows * group
    chunk = 2 * LANES
    slots_q = n * qrows // chunk
    units = slots_q * HALVES
    lane_rows = KV_HEADS // HALVES * chunk // LANES
    wq = (
        window_queries.reshape(query_rows, heads, HEAD_DIM)
        .transpose(1, 0, 2)
        .reshape(KV_HEADS, qrows, HEAD_DIM)
    )
    pool_scale = n * positions / (group * window * POOL)
    any_spec = pl.BlockSpec(memory_space=pl.ANY)
    vmem = pl.BlockSpec(memory_space=pltpu.VMEM)
    dma = pltpu.SemaphoreType.DMA
    A = n // 4
    f32, bf16 = jnp.float32, jnp.bfloat16
    importance, rows, score = pl.pallas_call(
        functools.partial(kernel, n, cap, cap_pad, pool_scale),
        out_shape=(
            jax.ShapeDtypeStruct((KV_HEADS, positions), f32),
            jax.ShapeDtypeStruct((n, cap_pad, 2 * HEAD_DIM), bf16),
            jax.ShapeDtypeStruct((n, 1, LANES), f32),
        ),
        in_specs=[any_spec] * 6,
        out_specs=(any_spec, any_spec, any_spec),
        scratch_shapes=[
            pltpu.VMEM((positions + 2 * EDGE, width), bf16),
            pltpu.VMEM((positions, width), bf16),
            pltpu.VMEM((KV_HEADS, slots_q, 2, 2, A // slots_q, qrows, HEAD_DIM), bf16),
            pltpu.VMEM((units, KV_HEADS // HALVES, positions, chunk), f32),
            pltpu.VMEM((units, KV_HEADS // HALVES, 16, chunk), f32),
            pltpu.VMEM((units, KV_HEADS // HALVES, positions // STRIP, 8, chunk), f32),
            pltpu.VMEM((KV_HEADS // HALVES, positions // STRIP, 8, chunk), f32),
            pltpu.VMEM((KV_HEADS, positions, LANES), f32),
            pltpu.VMEM((units, lane_rows, LANES), f32),
            pltpu.VMEM((units, 4, lane_rows, LANES), f32),
            pltpu.VMEM((units, n // 4, lane_rows, LANES), f32),
            pltpu.VMEM((n, cap_pad, 2 * HEAD_DIM), bf16),
            pltpu.VMEM((n * cap_pad // 2, positions), bf16),
            pltpu.VMEM((n, LANES), jnp.int32),
            pltpu.VMEM((n, LANES), jnp.int32),
            pltpu.VMEM((KV_HEADS, 1, positions), f32),
            pltpu.VMEM((16 * KV_HEADS, LANES), f32),
            pltpu.VMEM((n, 1, LANES), f32),
            pltpu.VMEM((KV_HEADS, positions), f32),
            pltpu.SMEM((1,), jnp.int32),
            pltpu.VMEM((slots,), jnp.int32),
            pltpu.VMEM((slots,), jnp.int32),
        ]
        + [dma((units,))] * 12
        + [dma((1,)), dma((1,)), dma((2,)), dma((2,)), dma((1,)), dma((1,)), dma((7,))],
        compiler_params=pltpu.CompilerParams(
            collective_id=0, has_side_effects=True, vmem_limit_bytes=60 * 1024 * 1024
        ),
        name="snap",
    )(cached_keys, cached_values, wq, kept_count, kept_entry, row_owner)
    importance, rows, score = pl.pallas_call(
        functools.partial(finish, cap),
        out_shape=(
            jax.ShapeDtypeStruct((KV_HEADS, positions), f32),
            jax.ShapeDtypeStruct((n, cap, 2 * HEAD_DIM), bf16),
            jax.ShapeDtypeStruct((n * cap,), bf16),
        ),
        in_specs=[vmem, vmem, vmem],
        out_specs=(vmem, vmem, vmem),
        name="finish",
    )(importance, rows, score)
    return importance, rows.reshape(n * cap, 2 * HEAD_DIM), score


def solution(mesh):
    n = mesh.shape["seq"]
    split = P(("rep", "seq"))
    wide = P(("rep", "seq"), None)
    return jax.shard_map(
        functools.partial(per_device, n),
        mesh=mesh,
        in_specs=(wide, wide, wide, split, split, split),
        out_specs=(P("rep", "seq"), wide, split),
        check_vma=False,
    )
```

```python
import functools

import jax
import jax.numpy as jnp
from jax import lax
from jax.experimental import pallas as pl
from jax.experimental.pallas import tpu as pltpu
from jax.sharding import PartitionSpec as P

KV_HEADS = 8
GROUP = 8
HEAD_DIM = 128
POOL = 7
LOG2E = 1.4426950408889634
LANES = 128
EDGE = 16
STRIP = 64
HALVES = 2
MESH = pl.DeviceIdType.MESH
NT = (((1,), (1,)), ((), ()))


def iota(shape, dim):
    return lax.broadcasted_iota(jnp.int32, shape, dim)


def kernel(
    n, cap, cap_pad, pool_scale,
    keys_hbm, vals_hbm, wq_hbm, count_hbm, entry_hbm, owner_hbm,
    imp_out, rows_out, score_out,
    keys, vals, qall, ebuf, raw, peak, sums, macc, stat, stat_x, stat_z, rows_send, onehot, slot_tile, slot_lane,
    mass, edge, ssend, imp_ref, count_ref, entry_ref, owner_ref,
    zs, zr, ws, wr, ys, yr, bs, br, xs, xr, qs, qr, rs, rr, hs, hr, ss, sr, ls,
):
    G = KV_HEADS
    me = lax.axis_index("seq")
    A = n // 4
    N, U = qall.shape[1], qall.shape[4]
    H = G // HALVES
    units = N * HALVES
    relay = U == 1 and N == 4
    a, b, c = me // 4, (me // 2) % 2, me % 2
    inner = a % U

    mine = a // U
    slots = entry_ref.shape[0]
    positions = vals.shape[0]
    tiles = positions // LANES
    out_slots = n * cap_pad
    chunk = ebuf.shape[3]
    scale2 = HEAD_DIM ** (-0.5) * LOG2E
    def to(index):
        return {"seq": index}

    def remote(src, dst, ssem, rsem, index):
        return pltpu.make_async_remote_copy(
            src_ref=src, dst_ref=dst, send_sem=ssem, recv_sem=rsem,
            device_id=to(index), device_id_type=MESH,
        )

    def drain(region, sem):
        pltpu.make_async_copy(region, region, sem).wait()

    low, high = lax.rem(me + n - 1, n), lax.rem(me + 1, n)
    mid_peer = a * 4 + (1 - b) * 2 + c
    core_peer = a * 4 + b * 2 + (1 - c)
    near, across = a + 1 - 2 * (a % 2), (a + 2) % A

    def hop_of(p):
        return jnp.where(a < 2, jnp.where(p == 0, 0, jnp.where(p == 3, 1, p + 1)), p)

    def unit_at(p):
        if not relay:
            return lax.rem(mine + p, N)
        hop = hop_of(p)
        return jnp.where(hop == 0, a, jnp.where(hop == 1, near, jnp.where(hop == 2, across, A - 1 - a)))

    def joined_at(p):
        return jnp.where(p < 2, p + 2, 3 - p) if relay else p


    def line_peer(k):
        return lax.rem(a + k, A) * 4 + b * 2 + c

    barrier = pltpu.get_barrier_semaphore()

    def announce(index):
        pl.semaphore_signal(barrier, inc=1, device_id=to(index), device_id_type=MESH)

    @pl.loop(1, A)
    def _(k):
        announce(line_peer(k))

    announce(mid_peer)
    announce(core_peer)

    @pl.when(me > 0)
    def _():
        announce(low)

    @pl.when(me < n - 1)
    def _():
        announce(high)

    own_q = pltpu.make_async_copy(wq_hbm, qall.at[:, mine, c, b, inner], ls.at[2])
    small = [
        pltpu.make_async_copy(src, dst, ls.at[4 + i])
        for i, (src, dst) in enumerate(((count_hbm, count_ref), (entry_hbm, entry_ref), (owner_hbm, owner_ref)))
    ]
    key_copy = pltpu.make_async_copy(keys_hbm, keys.at[pl.ds(0, positions)], ls.at[0])
    val_copy = pltpu.make_async_copy(vals_hbm, vals, ls.at[1])
    own_q.start()
    for copy in small:
        copy.start()
    key_copy.start()
    val_copy.start()

    first_rows = pl.ds(0, EDGE)
    last_rows = pl.ds(positions - EDGE, EDGE)
    from_low = pl.ds(positions, EDGE)
    from_high = pl.ds(positions + EDGE, EDGE)

    @pl.when(me == 0)
    def _():
        keys[positions:positions + EDGE, :] = jnp.zeros((EDGE, keys.shape[1]), keys.dtype)

    @pl.when(me == n - 1)
    def _():
        keys[positions + EDGE:positions + 2 * EDGE, :] = jnp.zeros((EDGE, keys.shape[1]), keys.dtype)

    def half(h):
        return pl.ds(h * H, H)

    def pieces(count):
        return qall.at[half(0)].reshape(H * N * 4 * U, qall.shape[5], HEAD_DIM).at[pl.ds(0, H * count)]

    def on_line(index):
        return index * 4 + b * 2 + c

    def greet():
        ends = jnp.where(me > 0, 1, 0) + jnp.where(me < n - 1, 1, 0)
        pl.semaphore_wait(barrier, A + 1 + ends)

        if U == 1:
            @pl.loop(0, HALVES)
            def _(h):
                k = mine * HALVES + h
                remote(wq_hbm.at[half(h)], qall.at[half(h), mine, c, b, inner], ys.at[k], yr.at[k], mid_peer).start()

        @pl.loop(0, HALVES)
        def _(h):
            piece, place, k = wq_hbm.at[half(h)], qall.at[half(h), mine, c, b, inner], mine * HALVES + h

            def send(index):
                remote(piece, place, zs.at[h], zr.at[k], on_line(index)).start()

            if relay:
                send(near)
                send(across)
            else:
                @pl.loop(1, A)
                def _(i):
                    send(lax.rem(a + i, A))

        @pl.when(me > 0)
        def _():
            remote(keys_hbm.at[first_rows], keys.at[from_high], hs.at[0], hr.at[0], low).start()

        @pl.when(me < n - 1)
        def _():
            remote(keys_hbm.at[last_rows], keys.at[from_low], hs.at[1], hr.at[1], high).start()

    reach = a + b
    late = reach > A // 2

    @pl.when(late)
    def _():
        greet()

    for copy in small:
        copy.wait()
    entry = entry_ref[...].reshape(1, slots)
    owner = owner_ref[...].reshape(1, slots)
    live = iota((1, slots), 1) < count_ref[0]
    owner_live = jnp.where(live, owner, -1)
    member = jnp.where(iota((n, slots), 0) == owner_live, 1.0, 0.0)
    before = jnp.where(iota((slots, slots), 0) < iota((slots, slots), 1), 1.0, 0.0).astype(jnp.bfloat16)
    earlier = jnp.dot(member.astype(jnp.bfloat16), before, preferred_element_type=jnp.float32)
    rank = jnp.sum(member * earlier, axis=0, keepdims=True).astype(jnp.int32)
    target = jnp.where(live, owner * cap_pad + rank, -1)
    tile_of = entry // LANES
    lane_of = entry - tile_of * LANES
    head = tile_of // tiles
    token_f = (entry - head * positions + 1).astype(jnp.float32)
    head_f = head.astype(jnp.float32)
    at_rank = jnp.where(iota((LANES, slots), 0) == rank, 1.0, 0.0).astype(jnp.bfloat16)

    def by_rank(value):
        marked = (member * value.astype(jnp.float32)).astype(jnp.bfloat16)
        return lax.dot_general(marked, at_rank, NT, preferred_element_type=jnp.float32).astype(jnp.int32)

    slot_tile[...] = by_rank(tile_of + 1)
    slot_lane[...] = by_rank(lane_of)

    @pl.when(reach == A // 2)
    def _():
        greet()

    key_copy.wait()
    val_copy.wait()

    def gather_rows(k0, count):
        blk = count * cap_pad
        hit = (iota((blk, slots), 0) + k0 * cap_pad) == target
        tok = jnp.sum(jnp.where(hit, token_f, 0.0), axis=1, keepdims=True).astype(jnp.int32) - 1
        hcol = jnp.sum(jnp.where(hit, head_f, 0.0), axis=1, keepdims=True).astype(jnp.int32)
        hcol = jnp.broadcast_to(hcol, (blk, HEAD_DIM))
        onehot[...] = jnp.where(iota((blk, positions), 1) == tok, 1.0, 0.0).astype(jnp.bfloat16)
        for side, source in enumerate((keys, vals)):
            got = jnp.dot(onehot[...], source[0:positions, :], preferred_element_type=jnp.float32)
            chosen = jnp.zeros((blk, HEAD_DIM), jnp.float32)
            for h in range(G):
                chosen = jnp.where(hcol == h, got[:, h * HEAD_DIM:(h + 1) * HEAD_DIM], chosen)
            for k in range(count):
                rows_send[k0 + k, :, side * HEAD_DIM:(side + 1) * HEAD_DIM] = chosen[
                    k * cap_pad:(k + 1) * cap_pad
                ].astype(jnp.bfloat16)

    per = onehot.shape[0] // cap_pad
    gather_rows(0, per)

    @pl.when(reach < A // 2)
    def _():
        greet()

    def lse(values):
        top = values[0]
        for x in values[1:]:
            top = jnp.maximum(top, x)
        total = jnp.zeros_like(top)
        for x in values:
            total = total + jnp.exp2(x - top)
        return top + jnp.log(total) * LOG2E

    chips = n // 2
    chip = me // 2

    def join_pair(i):
        g = unit_at(i // HALVES) * HALVES + i % HALVES
        drain(stat_x.at[g, pl.ds(0, 1)], xr.at[g])
        stat_z[g, chip] = lse([stat_x[g, d] for d in range(2)])

        @pl.loop(1, chips)
        def _(k):
            peer = lax.rem(chip + k, chips) * 2 + c
            remote(stat_z.at[g, chip], stat_z.at[g, chip], qs.at[g], qr.at[g], peer).start()

    strip = sums.shape[1]
    span = positions // strip
    columns = chunk // LANES

    def compute(r, h):
        k = r * HALVES + h
        for i in range(H):
            g = h * H + i
            group_q = qall.at[g, r].reshape(chunk, HEAD_DIM)
            key_cols = pl.ds(pl.multiple_of(g * HEAD_DIM, HEAD_DIM), HEAD_DIM)
            s = lax.dot_general(keys[:, key_cols], group_q[...], NT, preferred_element_type=jnp.float32)
            for u in range(strip):
                x = s[u * span:(u + 1) * span].reshape(span // 8, 8, chunk)
                top = jnp.max(x, axis=0)
                e = jnp.exp2((x - top[None]) * scale2)
                ebuf[k, i, u * span:(u + 1) * span, :] = e.reshape(span, chunk)
                peak[k, i, u] = top
                sums[i, u] = jnp.sum(e, axis=0)
            raw[k, i, 0:8, :] = s[positions + EDGE - 8:positions + EDGE]
            raw[k, i, 8:16, :] = s[positions + EDGE:positions + EDGE + 8]
        for i in range(H):
            tops = peak[k, i]
            top = jnp.max(jnp.max(tops, axis=0), axis=0, keepdims=True)
            total = jnp.sum(jnp.sum(sums[i] * jnp.exp2((tops - top[None]) * scale2), axis=0), axis=0, keepdims=True)
            local = top * scale2 + jnp.log(total) * LOG2E
            for j in range(columns):
                stat[k, i * columns + j:i * columns + j + 1, :] = local[:, j * LANES:(j + 1) * LANES]
        stat_x[k, c] = stat[k]
        remote(stat.at[k], stat_x.at[k, c], xs.at[k], xr.at[k], core_peer).start()

    own_rows = pltpu.make_async_copy(rows_send.at[me], rows_out.at[me], ls.at[3])
    lag = 2

    @pl.loop(0, G)
    def _(g):
        macc[g] = jnp.zeros(macc.shape[1:], jnp.float32)

    edge[...] = jnp.zeros(edge.shape, jnp.float32)

    def send_middle(i):
        p, h = i // HALVES, i % HALVES
        unit = unit_at(p)
        k = unit * HALVES + h
        block = qall.at[half(h), unit, c, b]

        @pl.when(p > 0)
        def _():
            drain(pieces(U), zr.at[k])

        if U > 1:
            @pl.when(p == 0)
            def _():
                drain(pieces(U - 1), zr.at[k])

            remote(block, block, ys.at[k], yr.at[k], mid_peer).start()
        else:
            @pl.when(p > 0)
            def _():
                remote(block, block, ys.at[k], yr.at[k], mid_peer).start()

        if relay:
            @pl.when(hop_of(p) == 2)
            def _():
                remote(block, block, ws.at[h], zr.at[k], on_line(near)).start()

    def send_core(i):
        h = i % HALVES
        unit = unit_at(i // HALVES)
        k = unit * HALVES + h
        drain(qall.at[half(h), unit, c, 1 - b], yr.at[k])
        block = qall.at[half(h), unit, c]
        remote(block, block, bs.at[k], br.at[k], core_peer).start()

    own_q.wait()
    if U > 1:
        for i in range(HALVES):
            send_middle(i)

    @pl.loop(0, units + 1)
    def _(step):
        @pl.when(step == 0)
        def _():
            gather_rows(per, per)
            own_rows.start()

        @pl.when((step > 0) & (step < units - 2))
        def _():
            send_middle(step + 2)

        @pl.when(step < units)
        def _():
            send_core(step)

        @pl.when(step == 0)
        def _():
            send_middle(step + 2)

        @pl.when((step == 1) & (me < n - 1))
        def _():
            drain(keys.at[from_high], hr.at[0])

        @pl.when((step == 1) & (me > 0))
        def _():
            drain(keys.at[from_low], hr.at[1])

        @pl.when(step >= 1)
        def _():
            h = (step - 1) % HALVES
            unit = unit_at((step - 1) // HALVES)
            drain(qall.at[half(h), unit, 1 - c], br.at[unit * HALVES + h])
            compute(unit, h)

        @pl.when(step >= lag)
        def _():
            join_pair(step - lag)

    join_pair(units - 1)

    @pl.loop(1, n)
    def _(k):
        peer = lax.rem(me + k, n)
        remote(rows_send.at[peer], rows_out.at[me], rs.at[0], rr.at[0], peer).start()

    @pl.loop(0, units)
    def _(i):
        h = i % HALVES
        k = joined_at(i // HALVES) * HALVES + h
        drain(stat_z.at[k, pl.ds(0, chips - 1)], qr.at[k])
        whole = lse([stat_z[k, d] for d in range(chips)])
        for j in range(H):
            g = h * H + j
            level = [whole[j * columns + d:j * columns + d + 1, :] for d in range(columns)]
            for u in range(strip):
                weight = [
                    jnp.exp2(peak[k, j, u, :, d * LANES:(d + 1) * LANES] * scale2 - level[d]) for d in range(columns)
                ]
                rows = slice(u * span, (u + 1) * span)
                acc = macc[g, rows, :].reshape(span // 8, 8, LANES)
                for d in range(columns):
                    e = ebuf[k, j, rows, d * LANES:(d + 1) * LANES].reshape(span // 8, 8, LANES)
                    acc = acc + e * weight[d][None]
                macc[g, rows, :] = acc.reshape(span, LANES)
            acc = edge[pl.ds(pl.multiple_of(g * 16, 16), 16), :]
            for d in range(columns):
                acc = acc + jnp.exp2(raw[k, j, :, d * LANES:(d + 1) * LANES] * scale2 - level[d])
            edge[pl.ds(pl.multiple_of(g * 16, 16), 16), :] = acc

        @pl.when(i >= units - HALVES)
        def _():
            for j in range(H):
                g = h * H + j
                for t in range(tiles):
                    acc = macc[g, t * LANES:(t + 1) * LANES, :]
                    mass[g, :, t * LANES:(t + 1) * LANES] = jnp.sum(acc.T, axis=0, keepdims=True)

    column = jnp.concatenate([mass[g] for g in range(G)], axis=0)
    line = jnp.sum(edge[...].T, axis=0, keepdims=True)
    row_of = iota((G, LANES), 0)
    ends = jnp.zeros((G, LANES), jnp.float32)
    for g in range(G):
        turned = pltpu.roll(line, (LANES - 8 - 16 * g) % LANES, 1)
        ends = jnp.where(row_of == g, turned, ends)
    before_low = jnp.where(me > 0, ends, 0.0)
    after_high = jnp.where(me < n - 1, ends, 0.0)
    padded = jnp.concatenate([before_low, column, after_high], axis=1)
    width = padded.shape[1]
    pooled = padded
    for o in range(1, POOL // 2 + 1):
        pooled = pooled + pltpu.roll(padded, o, 1) + pltpu.roll(padded, width - o, 1)
    importance = pooled[:, LANES:LANES + positions] * pool_scale
    imp_ref[...] = importance
    own_imp = pltpu.make_async_copy(imp_ref, imp_out, ls.at[2])
    own_imp.start()

    want, lane = slot_tile[...], slot_lane[...]
    table = jnp.zeros((n, LANES), jnp.float32)
    for h in range(G):
        for t in range(tiles):
            part = jnp.broadcast_to(importance[h:h + 1, t * LANES:(t + 1) * LANES], (n, LANES))
            found = jnp.take_along_axis(part, lane, axis=1)
            table = jnp.where(want == h * tiles + t + 1, found, table)
    for k in range(n):
        ssend[k] = table[k:k + 1, :]
    own_score = pltpu.make_async_copy(ssend.at[me], score_out.at[me], ls.at[0])
    own_score.start()

    @pl.loop(1, n)
    def _(k):
        peer = lax.rem(me + k, n)
        remote(ssend.at[peer], score_out.at[me], ss.at[0], sr.at[0], peer).start()

    own_rows.wait()
    drain(rows_out.at[pl.ds(0, n - 1)], rr.at[0])
    drain(rows_send.at[pl.ds(0, n - 1)], rs.at[0])

    @pl.loop(0, HALVES)
    def _(h):
        if relay:
            drain(pieces(2), zs.at[h])
            drain(pieces(1), ws.at[h])
        else:
            drain(pieces(A - 1), zs.at[h])

    @pl.loop(0, units)
    def _(k):
        r, h = k // HALVES, k % HALVES
        drain(qall.at[half(h), r, c, b], ys.at[k])
        drain(qall.at[half(h), r, c], bs.at[k])
        drain(stat_x.at[k, pl.ds(0, 1)], xs.at[k])
        drain(stat_z.at[k, pl.ds(0, chips - 1)], qs.at[k])

    @pl.when(me > 0)
    def _():
        drain(keys.at[from_high], hs.at[0])

    @pl.when(me < n - 1)
    def _():
        drain(keys.at[from_low], hs.at[1])

    drain(ssend.at[pl.ds(0, n - 1)], ss.at[0])
    own_imp.wait()
    own_score.wait()
    drain(score_out.at[pl.ds(0, n - 1)], sr.at[0])


def finish(cap, imp_in, rows_in, score_in, imp_ref, rows_ref, score_ref):
    n = rows_in.shape[0]
    imp_ref[...] = imp_in[...]
    rows_ref[...] = rows_in[:, 0:cap, :]
    table = jnp.concatenate([score_in[k] for k in range(n)], axis=0).astype(jnp.bfloat16)
    column = iota((LANES, n * cap), 1) - iota((LANES, n * cap), 0)
    unfold = jnp.where(column % cap == 0, 1.0, 0.0)
    unfold = jnp.where(iota((LANES, n * cap), 0) < cap, unfold, 0.0).astype(jnp.bfloat16)
    wide = jnp.dot(table, unfold, preferred_element_type=jnp.float32)
    within = iota((n, n * cap), 1) - iota((n, n * cap), 0) * cap
    line = jnp.sum(jnp.where((within >= 0) & (within < cap), wide, 0.0), axis=0, keepdims=True)
    score_ref[...] = line.astype(jnp.bfloat16).reshape(n * cap)


def per_device(n, cached_keys, cached_values, window_queries, kept_count, kept_entry, row_owner):
    positions, width = cached_keys.shape
    slots = kept_entry.shape[0]
    cap = slots // n
    cap_pad = -(-cap // 8) * 8
    query_rows = window_queries.shape[0]
    heads = window_queries.shape[1] // HEAD_DIM
    group = heads // KV_HEADS
    window = query_rows * n
    qrows = query_rows * group
    chunk = 2 * LANES
    slots_q = n * qrows // chunk
    units = slots_q * HALVES
    lane_rows = KV_HEADS // HALVES * chunk // LANES
    wq = (
        window_queries.reshape(query_rows, heads, HEAD_DIM)
        .transpose(1, 0, 2)
        .reshape(KV_HEADS, qrows, HEAD_DIM)
    )
    pool_scale = n * positions / (group * window * POOL)
    any_spec = pl.BlockSpec(memory_space=pl.ANY)
    vmem = pl.BlockSpec(memory_space=pltpu.VMEM)
    dma = pltpu.SemaphoreType.DMA
    A = n // 4
    f32, bf16 = jnp.float32, jnp.bfloat16
    importance, rows, score = pl.pallas_call(
        functools.partial(kernel, n, cap, cap_pad, pool_scale),
        out_shape=(
            jax.ShapeDtypeStruct((KV_HEADS, positions), f32),
            jax.ShapeDtypeStruct((n, cap_pad, 2 * HEAD_DIM), bf16),
            jax.ShapeDtypeStruct((n, 1, LANES), f32),
        ),
        in_specs=[any_spec] * 6,
        out_specs=(any_spec, any_spec, any_spec),
        scratch_shapes=[
            pltpu.VMEM((positions + 2 * EDGE, width), bf16),
            pltpu.VMEM((positions, width), bf16),
            pltpu.VMEM((KV_HEADS, slots_q, 2, 2, A // slots_q, qrows, HEAD_DIM), bf16),
            pltpu.VMEM((units, KV_HEADS // HALVES, positions, chunk), f32),
            pltpu.VMEM((units, KV_HEADS // HALVES, 16, chunk), f32),
            pltpu.VMEM((units, KV_HEADS // HALVES, positions // STRIP, 8, chunk), f32),
            pltpu.VMEM((KV_HEADS // HALVES, positions // STRIP, 8, chunk), f32),
            pltpu.VMEM((KV_HEADS, positions, LANES), f32),
            pltpu.VMEM((units, lane_rows, LANES), f32),
            pltpu.VMEM((units, 2, lane_rows, LANES), f32),
            pltpu.VMEM((units, n // 2, lane_rows, LANES), f32),
            pltpu.VMEM((n, cap_pad, 2 * HEAD_DIM), bf16),
            pltpu.VMEM((n * cap_pad // 2, positions), bf16),
            pltpu.VMEM((n, LANES), jnp.int32),
            pltpu.VMEM((n, LANES), jnp.int32),
            pltpu.VMEM((KV_HEADS, 1, positions), f32),
            pltpu.VMEM((16 * KV_HEADS, LANES), f32),
            pltpu.VMEM((n, 1, LANES), f32),
            pltpu.VMEM((KV_HEADS, positions), f32),
            pltpu.SMEM((1,), jnp.int32),
            pltpu.VMEM((slots,), jnp.int32),
            pltpu.VMEM((slots,), jnp.int32),
        ]
        + [dma((units,))] * 12
        + [dma((1,)), dma((1,)), dma((2,)), dma((2,)), dma((1,)), dma((1,)), dma((7,))],
        compiler_params=pltpu.CompilerParams(
            collective_id=0, has_side_effects=True, vmem_limit_bytes=60 * 1024 * 1024
        ),
        name="snap",
    )(cached_keys, cached_values, wq, kept_count, kept_entry, row_owner)
    importance, rows, score = pl.pallas_call(
        functools.partial(finish, cap),
        out_shape=(
            jax.ShapeDtypeStruct((KV_HEADS, positions), f32),
            jax.ShapeDtypeStruct((n, cap, 2 * HEAD_DIM), bf16),
            jax.ShapeDtypeStruct((n * cap,), bf16),
        ),
        in_specs=[vmem, vmem, vmem],
        out_specs=(vmem, vmem, vmem),
        name="finish",
    )(importance, rows, score)
    return importance, rows.reshape(n * cap, 2 * HEAD_DIM), score


def solution(mesh):
    n = mesh.shape["seq"]
    split = P(("rep", "seq"))
    wide = P(("rep", "seq"), None)
    return jax.shard_map(
        functools.partial(per_device, n),
        mesh=mesh,
        in_specs=(wide, wide, wide, split, split, split),
        out_specs=(P("rep", "seq"), wide, split),
        check_vma=False,
    )
```

```python
import functools

import jax
import jax.numpy as jnp
from jax import lax
from jax.experimental import pallas as pl
from jax.experimental.pallas import tpu as pltpu
from jax.sharding import PartitionSpec as P

KV_HEADS = 8
GROUP = 8
HEAD_DIM = 128
POOL = 7
LOG2E = 1.4426950408889634
LANES = 128
EDGE = 16
STRIP = 64
HALVES = 2
FAR_STEP = -1
MESH = pl.DeviceIdType.MESH
NT = (((1,), (1,)), ((), ()))


def iota(shape, dim):
    return lax.broadcasted_iota(jnp.int32, shape, dim)


def kernel(
    n, cap, cap_pad, pool_scale,
    keys_hbm, vals_hbm, wq_hbm, count_hbm, entry_hbm, owner_hbm,
    imp_out, rows_out, score_out,
    keys, vals, qall, ebuf, raw, peak, sums, macc, stat, stat_x, stat_z, rows_send, onehot, slot_tile, slot_lane,
    mass, edge, ssend, imp_ref, count_ref, entry_ref, owner_ref,
    zs, zr, ws, wr, ys, yr, bs, br, xs, xr, qs, qr, rs, rr, hs, hr, ss, sr, ls,
):
    G = KV_HEADS
    me = lax.axis_index("seq")
    A = n // 4
    N, U = qall.shape[1], qall.shape[4]
    H = G // HALVES
    units = N * HALVES
    relay = U == 1 and N == 4
    a, b, c = me // 4, (me // 2) % 2, me % 2
    inner = a % U

    mine = a // U
    slots = entry_ref.shape[0]
    positions = vals.shape[0]
    tiles = positions // LANES
    out_slots = n * cap_pad
    chunk = ebuf.shape[3]
    scale2 = HEAD_DIM ** (-0.5) * LOG2E
    def to(index):
        return {"seq": index}

    def remote(src, dst, ssem, rsem, index):
        return pltpu.make_async_remote_copy(
            src_ref=src, dst_ref=dst, send_sem=ssem, recv_sem=rsem,
            device_id=to(index), device_id_type=MESH,
        )

    def drain(region, sem):
        pltpu.make_async_copy(region, region, sem).wait()

    low, high = lax.rem(me + n - 1, n), lax.rem(me + 1, n)
    mid_peer = a * 4 + (1 - b) * 2 + c
    core_peer = a * 4 + b * 2 + (1 - c)
    near, across = a + 1 - 2 * (a % 2), (a + 2) % A

    def hop_of(p):
        return jnp.where(a < 2, jnp.where(p == 0, 0, jnp.where(p == 3, 1, p + 1)), p)

    def unit_at(p):
        if not relay:
            return lax.rem(mine + p, N)
        hop = hop_of(p)
        return jnp.where(hop == 0, a, jnp.where(hop == 1, near, jnp.where(hop == 2, across, A - 1 - a)))

    def joined_at(p):
        return jnp.where(p < 2, p + 2, 3 - p) if relay else p


    def line_peer(k):
        return lax.rem(a + k, A) * 4 + b * 2 + c

    barrier = pltpu.get_barrier_semaphore()

    def announce(index):
        pl.semaphore_signal(barrier, inc=1, device_id=to(index), device_id_type=MESH)

    @pl.loop(1, A)
    def _(k):
        announce(line_peer(k))

    announce(mid_peer)
    announce(core_peer)

    @pl.when(me > 0)
    def _():
        announce(low)

    @pl.when(me < n - 1)
    def _():
        announce(high)

    own_q = pltpu.make_async_copy(wq_hbm, qall.at[:, mine, c, b, inner], ls.at[2])
    small = [
        pltpu.make_async_copy(src, dst, ls.at[4 + i])
        for i, (src, dst) in enumerate(((count_hbm, count_ref), (entry_hbm, entry_ref), (owner_hbm, owner_ref)))
    ]
    key_copy = pltpu.make_async_copy(keys_hbm, keys.at[pl.ds(0, positions)], ls.at[0])
    val_copy = pltpu.make_async_copy(vals_hbm, vals, ls.at[1])
    own_q.start()
    for copy in small:
        copy.start()
    key_copy.start()
    val_copy.start()

    first_rows = pl.ds(0, EDGE)
    last_rows = pl.ds(positions - EDGE, EDGE)
    from_low = pl.ds(positions, EDGE)
    from_high = pl.ds(positions + EDGE, EDGE)

    @pl.when(me == 0)
    def _():
        keys[positions:positions + EDGE, :] = jnp.zeros((EDGE, keys.shape[1]), keys.dtype)

    @pl.when(me == n - 1)
    def _():
        keys[positions + EDGE:positions + 2 * EDGE, :] = jnp.zeros((EDGE, keys.shape[1]), keys.dtype)

    def half(h):
        return pl.ds(h * H, H)

    def pieces(count):
        return qall.at[half(0)].reshape(H * N * 4 * U, qall.shape[5], HEAD_DIM).at[pl.ds(0, H * count)]

    def on_line(index):
        return index * 4 + b * 2 + c

    def greet():
        ends = jnp.where(me > 0, 1, 0) + jnp.where(me < n - 1, 1, 0)
        pl.semaphore_wait(barrier, A + 1 + ends)

        if U == 1:
            @pl.loop(0, HALVES)
            def _(h):
                k = mine * HALVES + h
                remote(wq_hbm.at[half(h)], qall.at[half(h), mine, c, b, inner], ys.at[0], yr.at[k], mid_peer).start()

        @pl.loop(0, HALVES)
        def _(h):
            piece, place, k = wq_hbm.at[half(h)], qall.at[half(h), mine, c, b, inner], mine * HALVES + h

            def send(index):
                remote(piece, place, zs.at[0], zr.at[k], on_line(index)).start()

            if relay:
                send(near)
                send(across)
            else:
                @pl.loop(1, A)
                def _(i):
                    send(lax.rem(a + i, A))

        @pl.when(me > 0)
        def _():
            remote(keys_hbm.at[first_rows], keys.at[from_high], hs.at[0], hr.at[0], low).start()

        @pl.when(me < n - 1)
        def _():
            remote(keys_hbm.at[last_rows], keys.at[from_low], hs.at[1], hr.at[1], high).start()

    reach = a + b
    late = reach > A // 2

    @pl.when(late)
    def _():
        greet()

    for copy in small:
        copy.wait()
    entry = entry_ref[...].reshape(1, slots)
    owner = owner_ref[...].reshape(1, slots)
    live = iota((1, slots), 1) < count_ref[0]
    owner_live = jnp.where(live, owner, -1)
    member = jnp.where(iota((n, slots), 0) == owner_live, 1.0, 0.0)
    before = jnp.where(iota((slots, slots), 0) < iota((slots, slots), 1), 1.0, 0.0).astype(jnp.bfloat16)
    earlier = jnp.dot(member.astype(jnp.bfloat16), before, preferred_element_type=jnp.float32)
    rank = jnp.sum(member * earlier, axis=0, keepdims=True).astype(jnp.int32)
    target = jnp.where(live, owner * cap_pad + rank, -1)
    tile_of = entry // LANES
    lane_of = entry - tile_of * LANES
    head = tile_of // tiles
    token_f = (entry - head * positions + 1).astype(jnp.float32)
    head_f = head.astype(jnp.float32)
    at_rank = jnp.where(iota((LANES, slots), 0) == rank, 1.0, 0.0).astype(jnp.bfloat16)

    def by_rank(value):
        marked = (member * value.astype(jnp.float32)).astype(jnp.bfloat16)
        return lax.dot_general(marked, at_rank, NT, preferred_element_type=jnp.float32).astype(jnp.int32)

    slot_tile[...] = by_rank(tile_of + 1)
    slot_lane[...] = by_rank(lane_of)

    @pl.when(reach == A // 2)
    def _():
        greet()

    key_copy.wait()
    val_copy.wait()

    def gather_rows(k0, count):
        blk = count * cap_pad
        hit = (iota((blk, slots), 0) + k0 * cap_pad) == target
        tok = jnp.sum(jnp.where(hit, token_f, 0.0), axis=1, keepdims=True).astype(jnp.int32) - 1
        hcol = jnp.sum(jnp.where(hit, head_f, 0.0), axis=1, keepdims=True).astype(jnp.int32)
        hcol = jnp.broadcast_to(hcol, (blk, HEAD_DIM))
        onehot[...] = jnp.where(iota((blk, positions), 1) == tok, 1.0, 0.0).astype(jnp.bfloat16)
        for side, source in enumerate((keys, vals)):
            got = jnp.dot(onehot[...], source[0:positions, :], preferred_element_type=jnp.float32)
            chosen = jnp.zeros((blk, HEAD_DIM), jnp.float32)
            for h in range(G):
                chosen = jnp.where(hcol == h, got[:, h * HEAD_DIM:(h + 1) * HEAD_DIM], chosen)
            for k in range(count):
                rows_send[k0 + k, :, side * HEAD_DIM:(side + 1) * HEAD_DIM] = chosen[
                    k * cap_pad:(k + 1) * cap_pad
                ].astype(jnp.bfloat16)

    per = onehot.shape[0] // cap_pad
    gather_rows(0, per)

    @pl.when(reach < A // 2)
    def _():
        greet()

    def lse(values):
        top = values[0]
        for x in values[1:]:
            top = jnp.maximum(top, x)
        total = jnp.zeros_like(top)
        for x in values:
            total = total + jnp.exp2(x - top)
        return top + jnp.log(total) * LOG2E

    chips = n // 2
    chip = me // 2

    def join_pair(i):
        g = unit_at(i // HALVES) * HALVES + i % HALVES
        drain(stat_x.at[g, pl.ds(0, 1)], xr.at[g])
        stat_z[g, chip] = lse([stat_x[g, d] for d in range(2)])

        @pl.loop(1, chips)
        def _(k):
            peer = lax.rem(chip + k, chips) * 2 + c
            remote(stat_z.at[g, chip], stat_z.at[g, chip], qs.at[0], qr.at[g], peer).start()

    strip = sums.shape[1]
    span = positions // strip
    columns = chunk // LANES

    def compute(r, h):
        k = r * HALVES + h
        for i in range(H):
            g = h * H + i
            group_q = qall.at[g, r].reshape(chunk, HEAD_DIM)
            key_cols = pl.ds(pl.multiple_of(g * HEAD_DIM, HEAD_DIM), HEAD_DIM)
            s = lax.dot_general(keys[:, key_cols], group_q[...], NT, preferred_element_type=jnp.float32)
            for u in range(strip):
                x = s[u * span:(u + 1) * span].reshape(span // 8, 8, chunk)
                top = jnp.max(x, axis=0)
                e = jnp.exp2((x - top[None]) * scale2)
                ebuf[k, i, u * span:(u + 1) * span, :] = e.reshape(span, chunk)
                peak[k, i, u] = top
                sums[i, u] = jnp.sum(e, axis=0)
            raw[k, i, 0:8, :] = s[positions + EDGE - 8:positions + EDGE]
            raw[k, i, 8:16, :] = s[positions + EDGE:positions + EDGE + 8]
        for i in range(H):
            tops = peak[k, i]
            top = jnp.max(jnp.max(tops, axis=0), axis=0, keepdims=True)
            total = jnp.sum(jnp.sum(sums[i] * jnp.exp2((tops - top[None]) * scale2), axis=0), axis=0, keepdims=True)
            local = top * scale2 + jnp.log(total) * LOG2E
            for j in range(columns):
                stat[k, i * columns + j:i * columns + j + 1, :] = local[:, j * LANES:(j + 1) * LANES]
        stat_x[k, c] = stat[k]
        remote(stat.at[k], stat_x.at[k, c], xs.at[0], xr.at[k], core_peer).start()

    own_rows = pltpu.make_async_copy(rows_send.at[me], rows_out.at[me], ls.at[3])
    lag = 2

    @pl.loop(0, G)
    def _(g):
        macc[g] = jnp.zeros(macc.shape[1:], jnp.float32)

    edge[...] = jnp.zeros(edge.shape, jnp.float32)

    def send_middle(i):
        p, h = i // HALVES, i % HALVES
        unit = unit_at(p)
        k = unit * HALVES + h
        block = qall.at[half(h), unit, c, b]

        @pl.when(p > 0)
        def _():
            drain(pieces(U), zr.at[k])

        if U > 1:
            @pl.when(p == 0)
            def _():
                drain(pieces(U - 1), zr.at[k])

            remote(block, block, ys.at[0], yr.at[k], mid_peer).start()
        else:
            @pl.when(p > 0)
            def _():
                remote(block, block, ys.at[0], yr.at[k], mid_peer).start()

        if relay:
            @pl.when(hop_of(p) == 2)
            def _():
                remote(block, block, ws.at[0], zr.at[k], on_line(near)).start()

    def send_core(i):
        h = i % HALVES
        unit = unit_at(i // HALVES)
        k = unit * HALVES + h
        drain(qall.at[half(h), unit, c, 1 - b], yr.at[k])
        block = qall.at[half(h), unit, c]
        remote(block, block, bs.at[0], br.at[k], core_peer).start()

    own_q.wait()
    if U > 1:
        for i in range(HALVES):
            send_middle(i)

    side, place = me // (n // 2), me % (n // 2)

    def send_rows(peer):
        remote(rows_send.at[peer], rows_out.at[me], rs.at[0], rr.at[0], peer).start()

    def far_rows():
        @pl.loop(0, n // 2)
        def _(k):
            send_rows((1 - side) * (n // 2) + lax.rem(place + k, n // 2))

    def near_rows():
        @pl.loop(1, n // 2)
        def _(k):
            send_rows(side * (n // 2) + lax.rem(place + k, n // 2))

    @pl.loop(0, units + 1)
    def _(step):
        @pl.when(step == 0)
        def _():
            gather_rows(per, per)
            own_rows.start()

        @pl.when((step > 0) & (step < units - 2))
        def _():
            send_middle(step + 2)

        @pl.when(step < units)
        def _():
            send_core(step)

        @pl.when(step == 0)
        def _():
            send_middle(step + 2)

        @pl.when((step == 1) & (me < n - 1))
        def _():
            drain(keys.at[from_high], hr.at[0])

        @pl.when((step == 1) & (me > 0))
        def _():
            drain(keys.at[from_low], hr.at[1])

        @pl.when(step >= 1)
        def _():
            h = (step - 1) % HALVES
            unit = unit_at((step - 1) // HALVES)
            drain(qall.at[half(h), unit, 1 - c], br.at[unit * HALVES + h])
            compute(unit, h)

        @pl.when(step == FAR_STEP)
        def _():
            far_rows()

        @pl.when(step >= lag)
        def _():
            join_pair(step - lag)

    join_pair(units - 1)

    near_rows()
    far_rows()

    @pl.loop(0, units)
    def _(i):
        h = i % HALVES
        k = joined_at(i // HALVES) * HALVES + h
        drain(stat_z.at[k, pl.ds(0, chips - 1)], qr.at[k])
        whole = lse([stat_z[k, d] for d in range(chips)])
        for j in range(H):
            g = h * H + j
            level = [whole[j * columns + d:j * columns + d + 1, :] for d in range(columns)]
            for u in range(strip):
                weight = [
                    jnp.exp2(peak[k, j, u, :, d * LANES:(d + 1) * LANES] * scale2 - level[d]) for d in range(columns)
                ]
                rows = slice(u * span, (u + 1) * span)
                acc = macc[g, rows, :].reshape(span // 8, 8, LANES)
                for d in range(columns):
                    e = ebuf[k, j, rows, d * LANES:(d + 1) * LANES].reshape(span // 8, 8, LANES)
                    acc = acc + e * weight[d][None]
                macc[g, rows, :] = acc.reshape(span, LANES)
            acc = edge[pl.ds(pl.multiple_of(g * 16, 16), 16), :]
            for d in range(columns):
                acc = acc + jnp.exp2(raw[k, j, :, d * LANES:(d + 1) * LANES] * scale2 - level[d])
            edge[pl.ds(pl.multiple_of(g * 16, 16), 16), :] = acc

        @pl.when(i >= units - HALVES)
        def _():
            for j in range(H):
                g = h * H + j
                for t in range(tiles):
                    acc = macc[g, t * LANES:(t + 1) * LANES, :]
                    mass[g, :, t * LANES:(t + 1) * LANES] = jnp.sum(acc.T, axis=0, keepdims=True)

    column = jnp.concatenate([mass[g] for g in range(G)], axis=0)
    line = jnp.sum(edge[...].T, axis=0, keepdims=True)
    row_of = iota((G, LANES), 0)
    ends = jnp.zeros((G, LANES), jnp.float32)
    for g in range(G):
        turned = pltpu.roll(line, (LANES - 8 - 16 * g) % LANES, 1)
        ends = jnp.where(row_of == g, turned, ends)
    before_low = jnp.where(me > 0, ends, 0.0)
    after_high = jnp.where(me < n - 1, ends, 0.0)
    padded = jnp.concatenate([before_low, column, after_high], axis=1)
    width = padded.shape[1]
    pooled = padded
    for o in range(1, POOL // 2 + 1):
        pooled = pooled + pltpu.roll(padded, o, 1) + pltpu.roll(padded, width - o, 1)
    importance = pooled[:, LANES:LANES + positions] * pool_scale
    imp_ref[...] = importance
    own_imp = pltpu.make_async_copy(imp_ref, imp_out, ls.at[2])
    own_imp.start()

    want, lane = slot_tile[...], slot_lane[...]
    table = jnp.zeros((n, LANES), jnp.float32)
    for h in range(G):
        for t in range(tiles):
            part = jnp.broadcast_to(importance[h:h + 1, t * LANES:(t + 1) * LANES], (n, LANES))
            found = jnp.take_along_axis(part, lane, axis=1)
            table = jnp.where(want == h * tiles + t + 1, found, table)
    for k in range(n):
        ssend[k] = table[k:k + 1, :]
    own_score = pltpu.make_async_copy(ssend.at[me], score_out.at[me], ls.at[0])
    own_score.start()

    @pl.loop(1, n)
    def _(k):
        peer = lax.rem(me + k, n)
        remote(ssend.at[peer], score_out.at[me], ss.at[0], sr.at[0], peer).start()

    own_rows.wait()
    drain(rows_out.at[pl.ds(0, n - 1)], rr.at[0])
    drain(rows_send.at[pl.ds(0, n - 1)], rs.at[0])

    if relay:
        drain(pieces(2 * HALVES), zs.at[0])
        drain(pieces(HALVES), ws.at[0])
    else:
        drain(pieces((A - 1) * HALVES), zs.at[0])

    drain(pieces(units * U), ys.at[0])
    drain(pieces(2 * units * U), bs.at[0])
    drain(stat, xs.at[0])
    drain(stat_z.at[:, pl.ds(0, chips - 1)], qs.at[0])

    @pl.when(me > 0)
    def _():
        drain(keys.at[from_high], hs.at[0])

    @pl.when(me < n - 1)
    def _():
        drain(keys.at[from_low], hs.at[1])

    drain(ssend.at[pl.ds(0, n - 1)], ss.at[0])
    own_imp.wait()
    own_score.wait()
    drain(score_out.at[pl.ds(0, n - 1)], sr.at[0])


def finish(cap, imp_in, rows_in, score_in, imp_ref, rows_ref, score_ref):
    n = rows_in.shape[0]
    imp_ref[...] = imp_in[...]
    rows_ref[...] = rows_in[:, 0:cap, :]
    table = jnp.concatenate([score_in[k] for k in range(n)], axis=0).astype(jnp.bfloat16)
    column = iota((LANES, n * cap), 1) - iota((LANES, n * cap), 0)
    unfold = jnp.where(column % cap == 0, 1.0, 0.0)
    unfold = jnp.where(iota((LANES, n * cap), 0) < cap, unfold, 0.0).astype(jnp.bfloat16)
    wide = jnp.dot(table, unfold, preferred_element_type=jnp.float32)
    within = iota((n, n * cap), 1) - iota((n, n * cap), 0) * cap
    line = jnp.sum(jnp.where((within >= 0) & (within < cap), wide, 0.0), axis=0, keepdims=True)
    score_ref[...] = line.astype(jnp.bfloat16).reshape(n * cap)


def per_device(n, cached_keys, cached_values, window_queries, kept_count, kept_entry, row_owner):
    positions, width = cached_keys.shape
    slots = kept_entry.shape[0]
    cap = slots // n
    cap_pad = -(-cap // 8) * 8
    query_rows = window_queries.shape[0]
    heads = window_queries.shape[1] // HEAD_DIM
    group = heads // KV_HEADS
    window = query_rows * n
    qrows = query_rows * group
    chunk = 2 * LANES
    slots_q = n * qrows // chunk
    units = slots_q * HALVES
    lane_rows = KV_HEADS // HALVES * chunk // LANES
    wq = (
        window_queries.reshape(query_rows, heads, HEAD_DIM)
        .transpose(1, 0, 2)
        .reshape(KV_HEADS, qrows, HEAD_DIM)
    )
    pool_scale = n * positions / (group * window * POOL)
    any_spec = pl.BlockSpec(memory_space=pl.ANY)
    vmem = pl.BlockSpec(memory_space=pltpu.VMEM)
    dma = pltpu.SemaphoreType.DMA
    A = n // 4
    f32, bf16 = jnp.float32, jnp.bfloat16
    importance, rows, score = pl.pallas_call(
        functools.partial(kernel, n, cap, cap_pad, pool_scale),
        out_shape=(
            jax.ShapeDtypeStruct((KV_HEADS, positions), f32),
            jax.ShapeDtypeStruct((n, cap_pad, 2 * HEAD_DIM), bf16),
            jax.ShapeDtypeStruct((n, 1, LANES), f32),
        ),
        in_specs=[any_spec] * 6,
        out_specs=(any_spec, any_spec, any_spec),
        scratch_shapes=[
            pltpu.VMEM((positions + 2 * EDGE, width), bf16),
            pltpu.VMEM((positions, width), bf16),
            pltpu.VMEM((KV_HEADS, slots_q, 2, 2, A // slots_q, qrows, HEAD_DIM), bf16),
            pltpu.VMEM((units, KV_HEADS // HALVES, positions, chunk), f32),
            pltpu.VMEM((units, KV_HEADS // HALVES, 16, chunk), f32),
            pltpu.VMEM((units, KV_HEADS // HALVES, positions // STRIP, 8, chunk), f32),
            pltpu.VMEM((KV_HEADS // HALVES, positions // STRIP, 8, chunk), f32),
            pltpu.VMEM((KV_HEADS, positions, LANES), f32),
            pltpu.VMEM((units, lane_rows, LANES), f32),
            pltpu.VMEM((units, 2, lane_rows, LANES), f32),
            pltpu.VMEM((units, n // 2, lane_rows, LANES), f32),
            pltpu.VMEM((n, cap_pad, 2 * HEAD_DIM), bf16),
            pltpu.VMEM((n * cap_pad // 2, positions), bf16),
            pltpu.VMEM((n, LANES), jnp.int32),
            pltpu.VMEM((n, LANES), jnp.int32),
            pltpu.VMEM((KV_HEADS, 1, positions), f32),
            pltpu.VMEM((16 * KV_HEADS, LANES), f32),
            pltpu.VMEM((n, 1, LANES), f32),
            pltpu.VMEM((KV_HEADS, positions), f32),
            pltpu.SMEM((1,), jnp.int32),
            pltpu.VMEM((slots,), jnp.int32),
            pltpu.VMEM((slots,), jnp.int32),
        ]
        + [dma((1,)), dma((units,))] * 6
        + [dma((1,)), dma((1,)), dma((2,)), dma((2,)), dma((1,)), dma((1,)), dma((7,))],
        compiler_params=pltpu.CompilerParams(
            collective_id=0, has_side_effects=True, vmem_limit_bytes=60 * 1024 * 1024
        ),
        name="snap",
    )(cached_keys, cached_values, wq, kept_count, kept_entry, row_owner)
    importance, rows, score = pl.pallas_call(
        functools.partial(finish, cap),
        out_shape=(
            jax.ShapeDtypeStruct((KV_HEADS, positions), f32),
            jax.ShapeDtypeStruct((n, cap, 2 * HEAD_DIM), bf16),
            jax.ShapeDtypeStruct((n * cap,), bf16),
        ),
        in_specs=[vmem, vmem, vmem],
        out_specs=(vmem, vmem, vmem),
        name="finish",
    )(importance, rows, score)
    return importance, rows.reshape(n * cap, 2 * HEAD_DIM), score


def solution(mesh):
    n = mesh.shape["seq"]
    split = P(("rep", "seq"))
    wide = P(("rep", "seq"), None)
    return jax.shard_map(
        functools.partial(per_device, n),
        mesh=mesh,
        in_specs=(wide, wide, wide, split, split, split),
        out_specs=(P("rep", "seq"), wide, split),
        check_vma=False,
    )
```

```python
import functools

import jax
import jax.numpy as jnp
from jax import lax
from jax.experimental import pallas as pl
from jax.experimental.pallas import tpu as pltpu
from jax.sharding import PartitionSpec as P

KV_HEADS = 8
GROUP = 8
HEAD_DIM = 128
POOL = 7
LOG2E = 1.4426950408889634
LANES = 128
EDGE = 16
STRIP = 64
HALVES = 2
MESH = pl.DeviceIdType.MESH
NT = (((1,), (1,)), ((), ()))


def iota(shape, dim):
    return lax.broadcasted_iota(jnp.int32, shape, dim)


def kernel(
    n, cap, cap_pad, pool_scale,
    keys_hbm, vals_hbm, wq_hbm, count_hbm, entry_hbm, owner_hbm,
    imp_out, rows_out, score_out,
    keys, vals, qall, ebuf, raw, peak, sums, macc, stat, stat_x, stat_z, rows_send, onehot, slot_tile, slot_lane,
    mass, edge, ssend, imp_ref, count_ref, entry_ref, owner_ref,
    zs, zr, ws, wr, ys, yr, bs, br, xs, xr, qs, qr, rs, rr, hs, hr, ss, sr, ls,
):
    G = KV_HEADS
    me = lax.axis_index("seq")
    A = n // 4
    N, U = qall.shape[1], qall.shape[4]
    H = G // HALVES
    units = N * HALVES
    relay = U == 1 and N == 4
    a, b, c = me // 4, (me // 2) % 2, me % 2
    inner = a % U

    mine = a // U
    slots = entry_ref.shape[0]
    positions = vals.shape[0]
    tiles = positions // LANES
    out_slots = n * cap_pad
    chunk = ebuf.shape[3]
    scale2 = HEAD_DIM ** (-0.5) * LOG2E
    def to(index):
        return {"seq": index}

    def remote(src, dst, ssem, rsem, index):
        return pltpu.make_async_remote_copy(
            src_ref=src, dst_ref=dst, send_sem=ssem, recv_sem=rsem,
            device_id=to(index), device_id_type=MESH,
        )

    def drain(region, sem):
        pltpu.make_async_copy(region, region, sem).wait()

    low, high = lax.rem(me + n - 1, n), lax.rem(me + 1, n)
    mid_peer = a * 4 + (1 - b) * 2 + c
    core_peer = a * 4 + b * 2 + (1 - c)
    near, across = a + 1 - 2 * (a % 2), (a + 2) % A

    def hop_of(p):
        return jnp.where(a < 2, jnp.where(p == 0, 0, jnp.where(p == 3, 1, p + 1)), p)

    def unit_at(p):
        if not relay:
            return lax.rem(mine + p, N)
        hop = hop_of(p)
        return jnp.where(hop == 0, a, jnp.where(hop == 1, near, jnp.where(hop == 2, across, A - 1 - a)))

    def joined_at(p):
        return jnp.where(p < 2, p + 2, 3 - p) if relay else p


    def line_peer(k):
        return lax.rem(a + k, A) * 4 + b * 2 + c

    barrier = pltpu.get_barrier_semaphore()

    def announce(index):
        pl.semaphore_signal(barrier, inc=1, device_id=to(index), device_id_type=MESH)

    @pl.loop(1, A)
    def _(k):
        announce(line_peer(k))

    announce(mid_peer)
    announce(core_peer)

    @pl.when(me > 0)
    def _():
        announce(low)

    @pl.when(me < n - 1)
    def _():
        announce(high)

    own_q = pltpu.make_async_copy(wq_hbm, qall.at[:, mine, c, b, inner], ls.at[2])
    small = [
        pltpu.make_async_copy(src, dst, ls.at[4 + i])
        for i, (src, dst) in enumerate(((count_hbm, count_ref), (entry_hbm, entry_ref), (owner_hbm, owner_ref)))
    ]
    key_copy = pltpu.make_async_copy(keys_hbm, keys.at[pl.ds(0, positions)], ls.at[0])
    val_copy = pltpu.make_async_copy(vals_hbm, vals, ls.at[1])
    own_q.start()
    for copy in small:
        copy.start()
    key_copy.start()
    val_copy.start()

    first_rows = pl.ds(0, EDGE)
    last_rows = pl.ds(positions - EDGE, EDGE)
    from_low = pl.ds(positions, EDGE)
    from_high = pl.ds(positions + EDGE, EDGE)

    @pl.when(me == 0)
    def _():
        keys[positions:positions + EDGE, :] = jnp.zeros((EDGE, keys.shape[1]), keys.dtype)

    @pl.when(me == n - 1)
    def _():
        keys[positions + EDGE:positions + 2 * EDGE, :] = jnp.zeros((EDGE, keys.shape[1]), keys.dtype)

    def half(h):
        return pl.ds(h * H, H)

    def pieces(count):
        return qall.at[half(0)].reshape(H * N * 4 * U, qall.shape[5], HEAD_DIM).at[pl.ds(0, H * count)]

    def on_line(index):
        return index * 4 + b * 2 + c

    def send_own(h):
        piece, place, k = wq_hbm.at[half(h)], qall.at[half(h), mine, c, b, inner], mine * HALVES + h
        if U == 1:
            remote(piece, place, ys.at[0], yr.at[k], mid_peer).start()

        def send(index):
            remote(piece, place, zs.at[0], zr.at[k], on_line(index)).start()

        if relay:
            send(near)
            send(across)
        else:
            @pl.loop(1, A)
            def _(i):
                send(lax.rem(a + i, A))

    def greet():
        ends = jnp.where(me > 0, 1, 0) + jnp.where(me < n - 1, 1, 0)
        pl.semaphore_wait(barrier, A + 1 + ends)

        send_own(0)

        @pl.when(me > 0)
        def _():
            remote(keys_hbm.at[first_rows], keys.at[from_high], hs.at[0], hr.at[0], low).start()

        @pl.when(me < n - 1)
        def _():
            remote(keys_hbm.at[last_rows], keys.at[from_low], hs.at[1], hr.at[1], high).start()

    reach = a + b
    late = reach > A // 2

    @pl.when(late)
    def _():
        greet()

    for copy in small:
        copy.wait()
    entry = entry_ref[...].reshape(1, slots)
    owner = owner_ref[...].reshape(1, slots)
    live = iota((1, slots), 1) < count_ref[0]
    owner_live = jnp.where(live, owner, -1)
    member = jnp.where(iota((n, slots), 0) == owner_live, 1.0, 0.0)
    before = jnp.where(iota((slots, slots), 0) < iota((slots, slots), 1), 1.0, 0.0).astype(jnp.bfloat16)
    earlier = jnp.dot(member.astype(jnp.bfloat16), before, preferred_element_type=jnp.float32)
    rank = jnp.sum(member * earlier, axis=0, keepdims=True).astype(jnp.int32)
    target = jnp.where(live, owner * cap_pad + rank, -1)
    tile_of = entry // LANES
    lane_of = entry - tile_of * LANES
    head = tile_of // tiles
    token_f = (entry - head * positions + 1).astype(jnp.float32)
    head_f = head.astype(jnp.float32)
    at_rank = jnp.where(iota((LANES, slots), 0) == rank, 1.0, 0.0).astype(jnp.bfloat16)

    def by_rank(value):
        marked = (member * value.astype(jnp.float32)).astype(jnp.bfloat16)
        return lax.dot_general(marked, at_rank, NT, preferred_element_type=jnp.float32).astype(jnp.int32)

    slot_tile[...] = by_rank(tile_of + 1)
    slot_lane[...] = by_rank(lane_of)

    @pl.when(reach == A // 2)
    def _():
        greet()

    key_copy.wait()
    val_copy.wait()

    def gather_rows(k0, count):
        blk = count * cap_pad
        hit = (iota((blk, slots), 0) + k0 * cap_pad) == target
        tok = jnp.sum(jnp.where(hit, token_f, 0.0), axis=1, keepdims=True).astype(jnp.int32) - 1
        hcol = jnp.sum(jnp.where(hit, head_f, 0.0), axis=1, keepdims=True).astype(jnp.int32)
        hcol = jnp.broadcast_to(hcol, (blk, HEAD_DIM))
        onehot[...] = jnp.where(iota((blk, positions), 1) == tok, 1.0, 0.0).astype(jnp.bfloat16)
        for side, source in enumerate((keys, vals)):
            got = jnp.dot(onehot[...], source[0:positions, :], preferred_element_type=jnp.float32)
            chosen = jnp.zeros((blk, HEAD_DIM), jnp.float32)
            for h in range(G):
                chosen = jnp.where(hcol == h, got[:, h * HEAD_DIM:(h + 1) * HEAD_DIM], chosen)
            for k in range(count):
                rows_send[k0 + k, :, side * HEAD_DIM:(side + 1) * HEAD_DIM] = chosen[
                    k * cap_pad:(k + 1) * cap_pad
                ].astype(jnp.bfloat16)

    per = onehot.shape[0] // cap_pad
    @pl.when(reach >= A // 2)
    def _():
        send_own(1)

    gather_rows(0, per)

    @pl.when(reach < A // 2)
    def _():
        greet()

    def lse(values):
        top = values[0]
        for x in values[1:]:
            top = jnp.maximum(top, x)
        total = jnp.zeros_like(top)
        for x in values:
            total = total + jnp.exp2(x - top)
        return top + jnp.log(total) * LOG2E

    chips = n // 2
    chip = me // 2

    def join_pair(i):
        g = unit_at(i // HALVES) * HALVES + i % HALVES
        drain(stat_x.at[g, pl.ds(0, 1)], xr.at[g])
        stat_z[g, chip] = lse([stat_x[g, d] for d in range(2)])

        @pl.loop(1, chips)
        def _(k):
            peer = lax.rem(chip + k, chips) * 2 + c
            remote(stat_z.at[g, chip], stat_z.at[g, chip], qs.at[0], qr.at[g], peer).start()

    strip = sums.shape[1]
    span = positions // strip
    columns = chunk // LANES

    def compute(r, h):
        k = r * HALVES + h
        for i in range(H):
            g = h * H + i
            group_q = qall.at[g, r].reshape(chunk, HEAD_DIM)
            key_cols = pl.ds(pl.multiple_of(g * HEAD_DIM, HEAD_DIM), HEAD_DIM)
            s = lax.dot_general(keys[:, key_cols], group_q[...], NT, preferred_element_type=jnp.float32)
            for u in range(strip):
                x = s[u * span:(u + 1) * span].reshape(span // 8, 8, chunk)
                top = jnp.max(x, axis=0)
                e = jnp.exp2((x - top[None]) * scale2)
                ebuf[k, i, u * span:(u + 1) * span, :] = e.reshape(span, chunk)
                peak[k, i, u] = top
                sums[i, u] = jnp.sum(e, axis=0)
            raw[k, i, 0:8, :] = s[positions + EDGE - 8:positions + EDGE]
            raw[k, i, 8:16, :] = s[positions + EDGE:positions + EDGE + 8]
        for i in range(H):
            tops = peak[k, i]
            top = jnp.max(jnp.max(tops, axis=0), axis=0, keepdims=True)
            total = jnp.sum(jnp.sum(sums[i] * jnp.exp2((tops - top[None]) * scale2), axis=0), axis=0, keepdims=True)
            local = top * scale2 + jnp.log(total) * LOG2E
            for j in range(columns):
                stat[k, i * columns + j:i * columns + j + 1, :] = local[:, j * LANES:(j + 1) * LANES]
        stat_x[k, c] = stat[k]
        remote(stat.at[k], stat_x.at[k, c], xs.at[0], xr.at[k], core_peer).start()

    own_rows = pltpu.make_async_copy(rows_send.at[me], rows_out.at[me], ls.at[3])
    lag = 2

    @pl.loop(0, G)
    def _(g):
        macc[g] = jnp.zeros(macc.shape[1:], jnp.float32)

    edge[...] = jnp.zeros(edge.shape, jnp.float32)

    def send_middle(i):
        p, h = i // HALVES, i % HALVES
        unit = unit_at(p)
        k = unit * HALVES + h
        block = qall.at[half(h), unit, c, b]

        @pl.when(p > 0)
        def _():
            drain(pieces(U), zr.at[k])

        if U > 1:
            @pl.when(p == 0)
            def _():
                drain(pieces(U - 1), zr.at[k])

            remote(block, block, ys.at[0], yr.at[k], mid_peer).start()
        else:
            @pl.when(p > 0)
            def _():
                remote(block, block, ys.at[0], yr.at[k], mid_peer).start()

        if relay:
            @pl.when(hop_of(p) == 2)
            def _():
                remote(block, block, ws.at[0], zr.at[k], on_line(near)).start()

    def send_core(i):
        h = i % HALVES
        unit = unit_at(i // HALVES)
        k = unit * HALVES + h
        drain(qall.at[half(h), unit, c, 1 - b], yr.at[k])
        block = qall.at[half(h), unit, c]
        remote(block, block, bs.at[0], br.at[k], core_peer).start()

    own_q.wait()

    @pl.when(reach < A // 2)
    def _():
        send_own(1)

    if U > 1:
        for i in range(HALVES):
            send_middle(i)

    side, place = me // (n // 2), me % (n // 2)

    def send_rows(peer):
        remote(rows_send.at[peer], rows_out.at[me], rs.at[0], rr.at[0], peer).start()

    def far_rows():
        @pl.loop(0, n // 2)
        def _(k):
            send_rows((1 - side) * (n // 2) + lax.rem(place + k, n // 2))

    def near_rows():
        @pl.loop(1, n // 2)
        def _(k):
            send_rows(side * (n // 2) + lax.rem(place + k, n // 2))

    @pl.loop(0, units + 1)
    def _(step):
        @pl.when(step == 0)
        def _():
            gather_rows(per, per)
            own_rows.start()

        @pl.when((step > 0) & (step < units - 2))
        def _():
            send_middle(step + 2)

        @pl.when(step < units)
        def _():
            send_core(step)

        @pl.when(step == 0)
        def _():
            send_middle(step + 2)

        @pl.when((step == 1) & (me < n - 1))
        def _():
            drain(keys.at[from_high], hr.at[0])

        @pl.when((step == 1) & (me > 0))
        def _():
            drain(keys.at[from_low], hr.at[1])

        @pl.when(step >= 1)
        def _():
            h = (step - 1) % HALVES
            unit = unit_at((step - 1) // HALVES)
            drain(qall.at[half(h), unit, 1 - c], br.at[unit * HALVES + h])
            compute(unit, h)

        @pl.when(step >= lag)
        def _():
            join_pair(step - lag)

    join_pair(units - 1)

    near_rows()
    far_rows()

    @pl.loop(0, units)
    def _(i):
        h = i % HALVES
        k = joined_at(i // HALVES) * HALVES + h
        drain(stat_z.at[k, pl.ds(0, chips - 1)], qr.at[k])
        whole = lse([stat_z[k, d] for d in range(chips)])
        for j in range(H):
            g = h * H + j
            level = [whole[j * columns + d:j * columns + d + 1, :] for d in range(columns)]
            for u in range(strip):
                weight = [
                    jnp.exp2(peak[k, j, u, :, d * LANES:(d + 1) * LANES] * scale2 - level[d]) for d in range(columns)
                ]
                rows = slice(u * span, (u + 1) * span)
                acc = macc[g, rows, :].reshape(span // 8, 8, LANES)
                for d in range(columns):
                    e = ebuf[k, j, rows, d * LANES:(d + 1) * LANES].reshape(span // 8, 8, LANES)
                    acc = acc + e * weight[d][None]
                macc[g, rows, :] = acc.reshape(span, LANES)
            acc = edge[pl.ds(pl.multiple_of(g * 16, 16), 16), :]
            for d in range(columns):
                acc = acc + jnp.exp2(raw[k, j, :, d * LANES:(d + 1) * LANES] * scale2 - level[d])
            edge[pl.ds(pl.multiple_of(g * 16, 16), 16), :] = acc

        @pl.when(i >= units - HALVES)
        def _():
            for j in range(H):
                g = h * H + j
                for t in range(tiles):
                    acc = macc[g, t * LANES:(t + 1) * LANES, :]
                    mass[g, :, t * LANES:(t + 1) * LANES] = jnp.sum(acc.T, axis=0, keepdims=True)

    column = jnp.concatenate([mass[g] for g in range(G)], axis=0)
    line = jnp.sum(edge[...].T, axis=0, keepdims=True)
    row_of = iota((G, LANES), 0)
    ends = jnp.zeros((G, LANES), jnp.float32)
    for g in range(G):
        turned = pltpu.roll(line, (LANES - 8 - 16 * g) % LANES, 1)
        ends = jnp.where(row_of == g, turned, ends)
    before_low = jnp.where(me > 0, ends, 0.0)
    after_high = jnp.where(me < n - 1, ends, 0.0)
    padded = jnp.concatenate([before_low, column, after_high], axis=1)
    width = padded.shape[1]
    pooled = padded
    for o in range(1, POOL // 2 + 1):
        pooled = pooled + pltpu.roll(padded, o, 1) + pltpu.roll(padded, width - o, 1)
    importance = pooled[:, LANES:LANES + positions] * pool_scale
    imp_ref[...] = importance
    own_imp = pltpu.make_async_copy(imp_ref, imp_out, ls.at[2])
    own_imp.start()

    want, lane = slot_tile[...], slot_lane[...]
    table = jnp.zeros((n, LANES), jnp.float32)
    for h in range(G):
        for t in range(tiles):
            part = jnp.broadcast_to(importance[h:h + 1, t * LANES:(t + 1) * LANES], (n, LANES))
            found = jnp.take_along_axis(part, lane, axis=1)
            table = jnp.where(want == h * tiles + t + 1, found, table)
    for k in range(n):
        ssend[k] = table[k:k + 1, :]
    own_score = pltpu.make_async_copy(ssend.at[me], score_out.at[me], ls.at[0])
    own_score.start()

    @pl.loop(1, n)
    def _(k):
        peer = lax.rem(me + k, n)
        remote(ssend.at[peer], score_out.at[me], ss.at[0], sr.at[0], peer).start()

    own_rows.wait()
    drain(rows_out.at[pl.ds(0, n - 1)], rr.at[0])
    drain(rows_send.at[pl.ds(0, n - 1)], rs.at[0])

    if relay:
        drain(pieces(2 * HALVES), zs.at[0])
        drain(pieces(HALVES), ws.at[0])
    else:
        drain(pieces((A - 1) * HALVES), zs.at[0])

    drain(pieces(units * U), ys.at[0])
    drain(pieces(2 * units * U), bs.at[0])
    drain(stat, xs.at[0])
    drain(stat_z.at[:, pl.ds(0, chips - 1)], qs.at[0])

    @pl.when(me > 0)
    def _():
        drain(keys.at[from_high], hs.at[0])

    @pl.when(me < n - 1)
    def _():
        drain(keys.at[from_low], hs.at[1])

    drain(ssend.at[pl.ds(0, n - 1)], ss.at[0])
    own_imp.wait()
    own_score.wait()
    drain(score_out.at[pl.ds(0, n - 1)], sr.at[0])


def finish(cap, imp_in, rows_in, score_in, imp_ref, rows_ref, score_ref):
    n = rows_in.shape[0]
    imp_ref[...] = imp_in[...]
    rows_ref[...] = rows_in[:, 0:cap, :]
    table = jnp.concatenate([score_in[k] for k in range(n)], axis=0).astype(jnp.bfloat16)
    column = iota((LANES, n * cap), 1) - iota((LANES, n * cap), 0)
    unfold = jnp.where(column % cap == 0, 1.0, 0.0)
    unfold = jnp.where(iota((LANES, n * cap), 0) < cap, unfold, 0.0).astype(jnp.bfloat16)
    wide = jnp.dot(table, unfold, preferred_element_type=jnp.float32)
    within = iota((n, n * cap), 1) - iota((n, n * cap), 0) * cap
    line = jnp.sum(jnp.where((within >= 0) & (within < cap), wide, 0.0), axis=0, keepdims=True)
    score_ref[...] = line.astype(jnp.bfloat16).reshape(n * cap)


def per_device(n, cached_keys, cached_values, window_queries, kept_count, kept_entry, row_owner):
    positions, width = cached_keys.shape
    slots = kept_entry.shape[0]
    cap = slots // n
    cap_pad = -(-cap // 8) * 8
    query_rows = window_queries.shape[0]
    heads = window_queries.shape[1] // HEAD_DIM
    group = heads // KV_HEADS
    window = query_rows * n
    qrows = query_rows * group
    chunk = 2 * LANES
    slots_q = n * qrows // chunk
    units = slots_q * HALVES
    lane_rows = KV_HEADS // HALVES * chunk // LANES
    wq = (
        window_queries.reshape(query_rows, heads, HEAD_DIM)
        .transpose(1, 0, 2)
        .reshape(KV_HEADS, qrows, HEAD_DIM)
    )
    pool_scale = n * positions / (group * window * POOL)
    any_spec = pl.BlockSpec(memory_space=pl.ANY)
    vmem = pl.BlockSpec(memory_space=pltpu.VMEM)
    dma = pltpu.SemaphoreType.DMA
    A = n // 4
    f32, bf16 = jnp.float32, jnp.bfloat16
    importance, rows, score = pl.pallas_call(
        functools.partial(kernel, n, cap, cap_pad, pool_scale),
        out_shape=(
            jax.ShapeDtypeStruct((KV_HEADS, positions), f32),
            jax.ShapeDtypeStruct((n, cap_pad, 2 * HEAD_DIM), bf16),
            jax.ShapeDtypeStruct((n, 1, LANES), f32),
        ),
        in_specs=[any_spec] * 6,
        out_specs=(any_spec, any_spec, any_spec),
        scratch_shapes=[
            pltpu.VMEM((positions + 2 * EDGE, width), bf16),
            pltpu.VMEM((positions, width), bf16),
            pltpu.VMEM((KV_HEADS, slots_q, 2, 2, A // slots_q, qrows, HEAD_DIM), bf16),
            pltpu.VMEM((units, KV_HEADS // HALVES, positions, chunk), f32),
            pltpu.VMEM((units, KV_HEADS // HALVES, 16, chunk), f32),
            pltpu.VMEM((units, KV_HEADS // HALVES, positions // STRIP, 8, chunk), f32),
            pltpu.VMEM((KV_HEADS // HALVES, positions // STRIP, 8, chunk), f32),
            pltpu.VMEM((KV_HEADS, positions, LANES), f32),
            pltpu.VMEM((units, lane_rows, LANES), f32),
            pltpu.VMEM((units, 2, lane_rows, LANES), f32),
            pltpu.VMEM((units, n // 2, lane_rows, LANES), f32),
            pltpu.VMEM((n, cap_pad, 2 * HEAD_DIM), bf16),
            pltpu.VMEM((n * cap_pad // 2, positions), bf16),
            pltpu.VMEM((n, LANES), jnp.int32),
            pltpu.VMEM((n, LANES), jnp.int32),
            pltpu.VMEM((KV_HEADS, 1, positions), f32),
            pltpu.VMEM((16 * KV_HEADS, LANES), f32),
            pltpu.VMEM((n, 1, LANES), f32),
            pltpu.VMEM((KV_HEADS, positions), f32),
            pltpu.SMEM((1,), jnp.int32),
            pltpu.VMEM((slots,), jnp.int32),
            pltpu.VMEM((slots,), jnp.int32),
        ]
        + [dma((1,)), dma((units,))] * 6
        + [dma((1,)), dma((1,)), dma((2,)), dma((2,)), dma((1,)), dma((1,)), dma((7,))],
        compiler_params=pltpu.CompilerParams(
            collective_id=0, has_side_effects=True, vmem_limit_bytes=60 * 1024 * 1024
        ),
        name="snap",
    )(cached_keys, cached_values, wq, kept_count, kept_entry, row_owner)
    importance, rows, score = pl.pallas_call(
        functools.partial(finish, cap),
        out_shape=(
            jax.ShapeDtypeStruct((KV_HEADS, positions), f32),
            jax.ShapeDtypeStruct((n, cap, 2 * HEAD_DIM), bf16),
            jax.ShapeDtypeStruct((n * cap,), bf16),
        ),
        in_specs=[vmem, vmem, vmem],
        out_specs=(vmem, vmem, vmem),
        name="finish",
    )(importance, rows, score)
    return importance, rows.reshape(n * cap, 2 * HEAD_DIM), score


def solution(mesh):
    n = mesh.shape["seq"]
    split = P(("rep", "seq"))
    wide = P(("rep", "seq"), None)
    return jax.shard_map(
        functools.partial(per_device, n),
        mesh=mesh,
        in_specs=(wide, wide, wide, split, split, split),
        out_specs=(P("rep", "seq"), wide, split),
        check_vma=False,
    )
```

```python
import functools

import jax
import jax.numpy as jnp
from jax import lax
from jax.experimental import pallas as pl
from jax.experimental.pallas import tpu as pltpu
from jax.sharding import PartitionSpec as P

KV_HEADS = 8
GROUP = 8
HEAD_DIM = 128
POOL = 7
LOG2E = 1.4426950408889634
LANES = 128
EDGE = 16
STRIP = 64
HALVES = 2
MESH = pl.DeviceIdType.MESH
NT = (((1,), (1,)), ((), ()))


def iota(shape, dim):
    return lax.broadcasted_iota(jnp.int32, shape, dim)


def kernel(
    n, cap, cap_pad, pool_scale,
    keys_hbm, vals_hbm, wq_hbm, count_hbm, entry_hbm, owner_hbm,
    imp_out, rows_out, score_out,
    keys, vals, qall, ebuf, raw, peak, sums, macc, stat, stat_x, stat_z, rows_send, onehot, slot_tile, slot_lane,
    mass, edge, ssend, imp_ref, count_ref, entry_ref, owner_ref,
    zs, zr, ws, wr, ys, yr, bs, br, xs, xr, qs, qr, rs, rr, hs, hr, ss, sr, ls,
):
    G = KV_HEADS
    me = lax.axis_index("seq")
    A = n // 4
    N, U = qall.shape[1], qall.shape[4]
    H = G // HALVES
    units = N * HALVES
    relay = U == 1 and N == 4
    a, b, c = me // 4, (me // 2) % 2, me % 2
    inner = a % U

    mine = a // U
    slots = entry_ref.shape[0]
    positions = vals.shape[0]
    tiles = positions // LANES
    out_slots = n * cap_pad
    chunk = ebuf.shape[3]
    scale2 = HEAD_DIM ** (-0.5) * LOG2E
    def to(index):
        return {"seq": index}

    def remote(src, dst, ssem, rsem, index):
        return pltpu.make_async_remote_copy(
            src_ref=src, dst_ref=dst, send_sem=ssem, recv_sem=rsem,
            device_id=to(index), device_id_type=MESH,
        )

    def drain(region, sem):
        pltpu.make_async_copy(region, region, sem).wait()

    low, high = lax.rem(me + n - 1, n), lax.rem(me + 1, n)
    mid_peer = a * 4 + (1 - b) * 2 + c
    core_peer = a * 4 + b * 2 + (1 - c)
    near, across = a + 1 - 2 * (a % 2), (a + 2) % A

    def hop_of(p):
        return jnp.where(a < 2, jnp.where(p == 0, 0, jnp.where(p == 3, 1, p + 1)), p)

    def unit_at(p):
        if not relay:
            return lax.rem(mine + p, N)
        hop = hop_of(p)
        return jnp.where(hop == 0, a, jnp.where(hop == 1, near, jnp.where(hop == 2, across, A - 1 - a)))

    def joined_at(p):
        return jnp.where(p < 2, p + 2, 3 - p) if relay else p


    def line_peer(k):
        return lax.rem(a + k, A) * 4 + b * 2 + c

    barrier = pltpu.get_barrier_semaphore()

    def announce(index):
        pl.semaphore_signal(barrier, inc=1, device_id=to(index), device_id_type=MESH)

    @pl.loop(1, A)
    def _(k):
        announce(line_peer(k))

    announce(mid_peer)
    announce(core_peer)

    @pl.when(me > 0)
    def _():
        announce(low)

    @pl.when(me < n - 1)
    def _():
        announce(high)

    own_q = pltpu.make_async_copy(wq_hbm, qall.at[:, mine, c, b, inner], ls.at[2])
    small = [
        pltpu.make_async_copy(src, dst, ls.at[4 + i])
        for i, (src, dst) in enumerate(((count_hbm, count_ref), (entry_hbm, entry_ref), (owner_hbm, owner_ref)))
    ]
    key_copy = pltpu.make_async_copy(keys_hbm, keys.at[pl.ds(0, positions)], ls.at[0])
    val_copy = pltpu.make_async_copy(vals_hbm, vals, ls.at[1])
    own_q.start()
    for copy in small:
        copy.start()
    key_copy.start()
    val_copy.start()

    first_rows = pl.ds(0, EDGE)
    last_rows = pl.ds(positions - EDGE, EDGE)
    from_low = pl.ds(positions, EDGE)
    from_high = pl.ds(positions + EDGE, EDGE)

    @pl.when(me == 0)
    def _():
        keys[positions:positions + EDGE, :] = jnp.zeros((EDGE, keys.shape[1]), keys.dtype)

    @pl.when(me == n - 1)
    def _():
        keys[positions + EDGE:positions + 2 * EDGE, :] = jnp.zeros((EDGE, keys.shape[1]), keys.dtype)

    def half(h):
        return pl.ds(h * H, H)

    def pieces(count):
        return qall.at[half(0)].reshape(H * N * 4 * U, qall.shape[5], HEAD_DIM).at[pl.ds(0, H * count)]

    def on_line(index):
        return index * 4 + b * 2 + c

    def send_own(h):
        piece, place, k = wq_hbm.at[half(h)], qall.at[half(h), mine, c, b, inner], mine * HALVES + h
        if U == 1:
            remote(piece, place, ys.at[0], yr.at[k], mid_peer).start()

        def send(index):
            remote(piece, place, zs.at[0], zr.at[k], on_line(index)).start()

        if relay:
            send(jnp.where(a < 2, across, near))
            send(jnp.where(a < 2, near, across))
        else:
            @pl.loop(1, A)
            def _(i):
                send(lax.rem(a + i, A))

    def greet():
        ends = jnp.where(me > 0, 1, 0) + jnp.where(me < n - 1, 1, 0)
        pl.semaphore_wait(barrier, A + 1 + ends)

        send_own(0)

        @pl.when(me > 0)
        def _():
            remote(keys_hbm.at[first_rows], keys.at[from_high], hs.at[0], hr.at[0], low).start()

        @pl.when(me < n - 1)
        def _():
            remote(keys_hbm.at[last_rows], keys.at[from_low], hs.at[1], hr.at[1], high).start()

    reach = a + b
    late = reach > A // 2

    @pl.when(late)
    def _():
        greet()

    for copy in small:
        copy.wait()
    entry = entry_ref[...].reshape(1, slots)
    owner = owner_ref[...].reshape(1, slots)
    live = iota((1, slots), 1) < count_ref[0]
    owner_live = jnp.where(live, owner, -1)
    member = jnp.where(iota((n, slots), 0) == owner_live, 1.0, 0.0)
    before = jnp.where(iota((slots, slots), 0) < iota((slots, slots), 1), 1.0, 0.0).astype(jnp.bfloat16)
    earlier = jnp.dot(member.astype(jnp.bfloat16), before, preferred_element_type=jnp.float32)
    rank = jnp.sum(member * earlier, axis=0, keepdims=True).astype(jnp.int32)
    target = jnp.where(live, owner * cap_pad + rank, -1)
    tile_of = entry // LANES
    lane_of = entry - tile_of * LANES
    head = tile_of // tiles
    token_f = (entry - head * positions + 1).astype(jnp.float32)
    head_f = head.astype(jnp.float32)
    at_rank = jnp.where(iota((LANES, slots), 0) == rank, 1.0, 0.0).astype(jnp.bfloat16)

    def by_rank(value):
        marked = (member * value.astype(jnp.float32)).astype(jnp.bfloat16)
        return lax.dot_general(marked, at_rank, NT, preferred_element_type=jnp.float32).astype(jnp.int32)

    slot_tile[...] = by_rank(tile_of + 1)
    slot_lane[...] = by_rank(lane_of)

    @pl.when(reach == A // 2)
    def _():
        greet()

    key_copy.wait()
    val_copy.wait()

    def gather_rows(k0, count):
        blk = count * cap_pad
        hit = (iota((blk, slots), 0) + k0 * cap_pad) == target
        tok = jnp.sum(jnp.where(hit, token_f, 0.0), axis=1, keepdims=True).astype(jnp.int32) - 1
        hcol = jnp.sum(jnp.where(hit, head_f, 0.0), axis=1, keepdims=True).astype(jnp.int32)
        hcol = jnp.broadcast_to(hcol, (blk, HEAD_DIM))
        onehot[...] = jnp.where(iota((blk, positions), 1) == tok, 1.0, 0.0).astype(jnp.bfloat16)
        for side, source in enumerate((keys, vals)):
            got = jnp.dot(onehot[...], source[0:positions, :], preferred_element_type=jnp.float32)
            chosen = jnp.zeros((blk, HEAD_DIM), jnp.float32)
            for h in range(G):
                chosen = jnp.where(hcol == h, got[:, h * HEAD_DIM:(h + 1) * HEAD_DIM], chosen)
            for k in range(count):
                rows_send[k0 + k, :, side * HEAD_DIM:(side + 1) * HEAD_DIM] = chosen[
                    k * cap_pad:(k + 1) * cap_pad
                ].astype(jnp.bfloat16)

    per = onehot.shape[0] // cap_pad
    @pl.when(reach >= A // 2)
    def _():
        send_own(1)

    gather_rows(0, per)

    @pl.when(reach < A // 2)
    def _():
        greet()

    def lse(values):
        top = values[0]
        for x in values[1:]:
            top = jnp.maximum(top, x)
        total = jnp.zeros_like(top)
        for x in values:
            total = total + jnp.exp2(x - top)
        return top + jnp.log(total) * LOG2E

    chips = n // 2
    chip = me // 2

    def join_pair(i):
        g = unit_at(i // HALVES) * HALVES + i % HALVES
        drain(stat_x.at[g, pl.ds(0, 1)], xr.at[g])
        stat_z[g, chip] = lse([stat_x[g, d] for d in range(2)])

        @pl.loop(1, chips)
        def _(k):
            peer = lax.rem(chip + k, chips) * 2 + c
            remote(stat_z.at[g, chip], stat_z.at[g, chip], qs.at[0], qr.at[g], peer).start()

    strip = sums.shape[1]
    span = positions // strip
    columns = chunk // LANES

    def compute(r, h):
        k = r * HALVES + h
        for i in range(H):
            g = h * H + i
            group_q = qall.at[g, r].reshape(chunk, HEAD_DIM)
            key_cols = pl.ds(pl.multiple_of(g * HEAD_DIM, HEAD_DIM), HEAD_DIM)
            s = lax.dot_general(keys[:, key_cols], group_q[...], NT, preferred_element_type=jnp.float32)
            for u in range(strip):
                x = s[u * span:(u + 1) * span].reshape(span // 8, 8, chunk)
                top = jnp.max(x, axis=0)
                e = jnp.exp2((x - top[None]) * scale2)
                ebuf[k, i, u * span:(u + 1) * span, :] = e.reshape(span, chunk)
                peak[k, i, u] = top
                sums[i, u] = jnp.sum(e, axis=0)
            raw[k, i, 0:8, :] = s[positions + EDGE - 8:positions + EDGE]
            raw[k, i, 8:16, :] = s[positions + EDGE:positions + EDGE + 8]
        for i in range(H):
            tops = peak[k, i]
            top = jnp.max(jnp.max(tops, axis=0), axis=0, keepdims=True)
            total = jnp.sum(jnp.sum(sums[i] * jnp.exp2((tops - top[None]) * scale2), axis=0), axis=0, keepdims=True)
            local = top * scale2 + jnp.log(total) * LOG2E
            for j in range(columns):
                stat[k, i * columns + j:i * columns + j + 1, :] = local[:, j * LANES:(j + 1) * LANES]
        stat_x[k, c] = stat[k]
        remote(stat.at[k], stat_x.at[k, c], xs.at[0], xr.at[k], core_peer).start()

    own_rows = pltpu.make_async_copy(rows_send.at[me], rows_out.at[me], ls.at[3])
    lag = 2

    @pl.loop(0, G)
    def _(g):
        macc[g] = jnp.zeros(macc.shape[1:], jnp.float32)

    edge[...] = jnp.zeros(edge.shape, jnp.float32)

    def send_middle(i):
        p, h = i // HALVES, i % HALVES
        unit = unit_at(p)
        k = unit * HALVES + h
        block = qall.at[half(h), unit, c, b]

        @pl.when(p > 0)
        def _():
            drain(pieces(U), zr.at[k])

        if U > 1:
            @pl.when(p == 0)
            def _():
                drain(pieces(U - 1), zr.at[k])

            remote(block, block, ys.at[0], yr.at[k], mid_peer).start()
        else:
            @pl.when(p > 0)
            def _():
                remote(block, block, ys.at[0], yr.at[k], mid_peer).start()

        if relay:
            @pl.when(hop_of(p) == 2)
            def _():
                remote(block, block, ws.at[0], zr.at[k], on_line(near)).start()

    def send_core(i):
        h = i % HALVES
        unit = unit_at(i // HALVES)
        k = unit * HALVES + h
        drain(qall.at[half(h), unit, c, 1 - b], yr.at[k])
        block = qall.at[half(h), unit, c]
        remote(block, block, bs.at[0], br.at[k], core_peer).start()

    own_q.wait()

    @pl.when(reach < A // 2)
    def _():
        send_own(1)

    if U > 1:
        for i in range(HALVES):
            send_middle(i)

    side, place = me // (n // 2), me % (n // 2)

    def send_rows(peer):
        remote(rows_send.at[peer], rows_out.at[me], rs.at[0], rr.at[0], peer).start()

    def far_rows():
        @pl.loop(0, n // 2)
        def _(k):
            send_rows((1 - side) * (n // 2) + lax.rem(place + k, n // 2))

    def near_rows():
        @pl.loop(1, n // 2)
        def _(k):
            send_rows(side * (n // 2) + lax.rem(place + k, n // 2))

    @pl.loop(0, units + 1)
    def _(step):
        @pl.when(step == 0)
        def _():
            gather_rows(per, per)
            own_rows.start()

        @pl.when((step > 0) & (step < units - 2))
        def _():
            send_middle(step + 2)

        @pl.when(step < units)
        def _():
            send_core(step)

        @pl.when(step == 0)
        def _():
            send_middle(step + 2)

        @pl.when((step == 1) & (me < n - 1))
        def _():
            drain(keys.at[from_high], hr.at[0])

        @pl.when((step == 1) & (me > 0))
        def _():
            drain(keys.at[from_low], hr.at[1])

        @pl.when(step >= 1)
        def _():
            h = (step - 1) % HALVES
            unit = unit_at((step - 1) // HALVES)
            drain(qall.at[half(h), unit, 1 - c], br.at[unit * HALVES + h])
            compute(unit, h)

        @pl.when(step >= lag)
        def _():
            join_pair(step - lag)

    join_pair(units - 1)

    near_rows()
    far_rows()

    @pl.loop(0, units)
    def _(i):
        h = i % HALVES
        k = joined_at(i // HALVES) * HALVES + h
        drain(stat_z.at[k, pl.ds(0, chips - 1)], qr.at[k])
        whole = lse([stat_z[k, d] for d in range(chips)])
        for j in range(H):
            g = h * H + j
            level = [whole[j * columns + d:j * columns + d + 1, :] for d in range(columns)]
            for u in range(strip):
                weight = [
                    jnp.exp2(peak[k, j, u, :, d * LANES:(d + 1) * LANES] * scale2 - level[d]) for d in range(columns)
                ]
                rows = slice(u * span, (u + 1) * span)
                acc = macc[g, rows, :].reshape(span // 8, 8, LANES)
                for d in range(columns):
                    e = ebuf[k, j, rows, d * LANES:(d + 1) * LANES].reshape(span // 8, 8, LANES)
                    acc = acc + e * weight[d][None]
                macc[g, rows, :] = acc.reshape(span, LANES)
            acc = edge[pl.ds(pl.multiple_of(g * 16, 16), 16), :]
            for d in range(columns):
                acc = acc + jnp.exp2(raw[k, j, :, d * LANES:(d + 1) * LANES] * scale2 - level[d])
            edge[pl.ds(pl.multiple_of(g * 16, 16), 16), :] = acc

        @pl.when(i >= units - HALVES)
        def _():
            for j in range(H):
                g = h * H + j
                for t in range(tiles):
                    acc = macc[g, t * LANES:(t + 1) * LANES, :]
                    mass[g, :, t * LANES:(t + 1) * LANES] = jnp.sum(acc.T, axis=0, keepdims=True)

    column = jnp.concatenate([mass[g] for g in range(G)], axis=0)
    line = jnp.sum(edge[...].T, axis=0, keepdims=True)
    row_of = iota((G, LANES), 0)
    ends = jnp.zeros((G, LANES), jnp.float32)
    for g in range(G):
        turned = pltpu.roll(line, (LANES - 8 - 16 * g) % LANES, 1)
        ends = jnp.where(row_of == g, turned, ends)
    before_low = jnp.where(me > 0, ends, 0.0)
    after_high = jnp.where(me < n - 1, ends, 0.0)
    padded = jnp.concatenate([before_low, column, after_high], axis=1)
    width = padded.shape[1]
    pooled = padded
    for o in range(1, POOL // 2 + 1):
        pooled = pooled + pltpu.roll(padded, o, 1) + pltpu.roll(padded, width - o, 1)
    importance = pooled[:, LANES:LANES + positions] * pool_scale
    imp_ref[...] = importance
    own_imp = pltpu.make_async_copy(imp_ref, imp_out, ls.at[2])
    own_imp.start()

    want, lane = slot_tile[...], slot_lane[...]
    table = jnp.zeros((n, LANES), jnp.float32)
    for h in range(G):
        for t in range(tiles):
            part = jnp.broadcast_to(importance[h:h + 1, t * LANES:(t + 1) * LANES], (n, LANES))
            found = jnp.take_along_axis(part, lane, axis=1)
            table = jnp.where(want == h * tiles + t + 1, found, table)
    for k in range(n):
        ssend[k] = table[k:k + 1, :]
    own_score = pltpu.make_async_copy(ssend.at[me], score_out.at[me], ls.at[0])
    own_score.start()

    @pl.loop(1, n)
    def _(k):
        peer = lax.rem(me + k, n)
        remote(ssend.at[peer], score_out.at[me], ss.at[0], sr.at[0], peer).start()

    own_rows.wait()
    drain(rows_out.at[pl.ds(0, n - 1)], rr.at[0])
    drain(rows_send.at[pl.ds(0, n - 1)], rs.at[0])

    if relay:
        drain(pieces(2 * HALVES), zs.at[0])
        drain(pieces(HALVES), ws.at[0])
    else:
        drain(pieces((A - 1) * HALVES), zs.at[0])

    drain(pieces(units * U), ys.at[0])
    drain(pieces(2 * units * U), bs.at[0])
    drain(stat, xs.at[0])
    drain(stat_z.at[:, pl.ds(0, chips - 1)], qs.at[0])

    @pl.when(me > 0)
    def _():
        drain(keys.at[from_high], hs.at[0])

    @pl.when(me < n - 1)
    def _():
        drain(keys.at[from_low], hs.at[1])

    drain(ssend.at[pl.ds(0, n - 1)], ss.at[0])
    own_imp.wait()
    own_score.wait()
    drain(score_out.at[pl.ds(0, n - 1)], sr.at[0])


def finish(cap, imp_in, rows_in, score_in, imp_ref, rows_ref, score_ref):
    n = rows_in.shape[0]
    imp_ref[...] = imp_in[...]
    rows_ref[...] = rows_in[:, 0:cap, :]
    table = jnp.concatenate([score_in[k] for k in range(n)], axis=0).astype(jnp.bfloat16)
    column = iota((LANES, n * cap), 1) - iota((LANES, n * cap), 0)
    unfold = jnp.where(column % cap == 0, 1.0, 0.0)
    unfold = jnp.where(iota((LANES, n * cap), 0) < cap, unfold, 0.0).astype(jnp.bfloat16)
    wide = jnp.dot(table, unfold, preferred_element_type=jnp.float32)
    within = iota((n, n * cap), 1) - iota((n, n * cap), 0) * cap
    line = jnp.sum(jnp.where((within >= 0) & (within < cap), wide, 0.0), axis=0, keepdims=True)
    score_ref[...] = line.astype(jnp.bfloat16).reshape(n * cap)


def per_device(n, cached_keys, cached_values, window_queries, kept_count, kept_entry, row_owner):
    positions, width = cached_keys.shape
    slots = kept_entry.shape[0]
    cap = slots // n
    cap_pad = -(-cap // 8) * 8
    query_rows = window_queries.shape[0]
    heads = window_queries.shape[1] // HEAD_DIM
    group = heads // KV_HEADS
    window = query_rows * n
    qrows = query_rows * group
    chunk = 2 * LANES
    slots_q = n * qrows // chunk
    units = slots_q * HALVES
    lane_rows = KV_HEADS // HALVES * chunk // LANES
    wq = (
        window_queries.reshape(query_rows, heads, HEAD_DIM)
        .transpose(1, 0, 2)
        .reshape(KV_HEADS, qrows, HEAD_DIM)
    )
    pool_scale = n * positions / (group * window * POOL)
    any_spec = pl.BlockSpec(memory_space=pl.ANY)
    vmem = pl.BlockSpec(memory_space=pltpu.VMEM)
    dma = pltpu.SemaphoreType.DMA
    A = n // 4
    f32, bf16 = jnp.float32, jnp.bfloat16
    importance, rows, score = pl.pallas_call(
        functools.partial(kernel, n, cap, cap_pad, pool_scale),
        out_shape=(
            jax.ShapeDtypeStruct((KV_HEADS, positions), f32),
            jax.ShapeDtypeStruct((n, cap_pad, 2 * HEAD_DIM), bf16),
            jax.ShapeDtypeStruct((n, 1, LANES), f32),
        ),
        in_specs=[any_spec] * 6,
        out_specs=(any_spec, any_spec, any_spec),
        scratch_shapes=[
            pltpu.VMEM((positions + 2 * EDGE, width), bf16),
            pltpu.VMEM((positions, width), bf16),
            pltpu.VMEM((KV_HEADS, slots_q, 2, 2, A // slots_q, qrows, HEAD_DIM), bf16),
            pltpu.VMEM((units, KV_HEADS // HALVES, positions, chunk), f32),
            pltpu.VMEM((units, KV_HEADS // HALVES, 16, chunk), f32),
            pltpu.VMEM((units, KV_HEADS // HALVES, positions // STRIP, 8, chunk), f32),
            pltpu.VMEM((KV_HEADS // HALVES, positions // STRIP, 8, chunk), f32),
            pltpu.VMEM((KV_HEADS, positions, LANES), f32),
            pltpu.VMEM((units, lane_rows, LANES), f32),
            pltpu.VMEM((units, 2, lane_rows, LANES), f32),
            pltpu.VMEM((units, n // 2, lane_rows, LANES), f32),
            pltpu.VMEM((n, cap_pad, 2 * HEAD_DIM), bf16),
            pltpu.VMEM((n * cap_pad // 2, positions), bf16),
            pltpu.VMEM((n, LANES), jnp.int32),
            pltpu.VMEM((n, LANES), jnp.int32),
            pltpu.VMEM((KV_HEADS, 1, positions), f32),
            pltpu.VMEM((16 * KV_HEADS, LANES), f32),
            pltpu.VMEM((n, 1, LANES), f32),
            pltpu.VMEM((KV_HEADS, positions), f32),
            pltpu.SMEM((1,), jnp.int32),
            pltpu.VMEM((slots,), jnp.int32),
            pltpu.VMEM((slots,), jnp.int32),
        ]
        + [dma((1,)), dma((units,))] * 6
        + [dma((1,)), dma((1,)), dma((2,)), dma((2,)), dma((1,)), dma((1,)), dma((7,))],
        compiler_params=pltpu.CompilerParams(
            collective_id=0, has_side_effects=True, vmem_limit_bytes=60 * 1024 * 1024
        ),
        name="snap",
    )(cached_keys, cached_values, wq, kept_count, kept_entry, row_owner)
    importance, rows, score = pl.pallas_call(
        functools.partial(finish, cap),
        out_shape=(
            jax.ShapeDtypeStruct((KV_HEADS, positions), f32),
            jax.ShapeDtypeStruct((n, cap, 2 * HEAD_DIM), bf16),
            jax.ShapeDtypeStruct((n * cap,), bf16),
        ),
        in_specs=[vmem, vmem, vmem],
        out_specs=(vmem, vmem, vmem),
        name="finish",
    )(importance, rows, score)
    return importance, rows.reshape(n * cap, 2 * HEAD_DIM), score


def solution(mesh):
    n = mesh.shape["seq"]
    split = P(("rep", "seq"))
    wide = P(("rep", "seq"), None)
    return jax.shard_map(
        functools.partial(per_device, n),
        mesh=mesh,
        in_specs=(wide, wide, wide, split, split, split),
        out_specs=(P("rep", "seq"), wide, split),
        check_vma=False,
    )
```
